256 devices in a mesh: row: 16 (over y, x), col: 8 (over z), chan: 2 (over core).
Axes of the slice: x: 4, y: 4, z: 8, core: 2. Of those that a mesh axis runs over, the one named last changes fastest.
Arguments:
- samples: bfloat16 [8192, 2, 8192], P(('chan', 'col'), None, 'row'), parts along dimension 0, may hold values from -6 to 6
- sky_model: bfloat16 [8192, 2, 4096], P(('chan', 'row'), None, 'col'), parts along dimension 0, may hold values from -128 to 128, as said below
- initial_gains: float32 [2, 8192], P(None, ('chan', 'row', 'col')), parts along dimension 1, may hold values from -3 to 3, as said below
Outputs:
- calibrated: float32 [2, 8192], P(None, ('chan', 'row', 'col')), parts along dimension 1
The draws below stay inside these ranges and needn't reach their ends.
There are 2 independent parts, one for each index of `chan`. The reference program is written for one: setup_inputs(seed, part) draws one part's arguments, and reference() takes and returns one part's arrays. A program takes and returns all parts, laid end to end along the dimension named above; each array names one. Nothing has to cross between parts.
Inputs may be any that keep to these rules, and one draw needn't show every extreme that they name: sky_model is Hermitian: sky_model[q,0,p] = sky_model[p,0,q] and sky_model[q,1,p] = -sky_model[p,1,q]. `initial_gains`: every initial gain has magnitude between 0.3 and 3.
All inputs are finite; a program needn't handle non-finite values.
Results may differ from the reference program's by a relative error of at most 0.0003.
Values may be sent and summed in bfloat16 or wider, within the bound.
No kernel may reach another device: no remote copies, remote signals or barrier semaphores. Data moves between devices by JAX's collectives and lax.ppermute only.
A program may use at most 192 MiB of HBM per device.

```python
import math
import jax
import jax.numpy as jnp
from jax import lax

ANTENNA_NUMBER = 4096
ITERS = 3
TIME_SAMPLES = 8192


def antenna_scales(key):
    lower_limit = 0.5
    upper_limit = 2.0
    linear_ramp = 1.0 + 2.0 * jnp.arange(ANTENNA_NUMBER, dtype=jnp.float32) / max(ANTENNA_NUMBER - 1, 1)
    gain_spread = jnp.exp(jax.random.uniform(key, (ANTENNA_NUMBER,), jnp.float32, math.log(lower_limit), math.log(upper_limit)))
    return linear_ramp * gain_spread


def draw_sky_model(key, part):
    primary_key, secondary_key = jax.random.split(jax.random.fold_in(key, 11))
    scales = antenna_scales(primary_key)
    baseline_level = jax.random.truncated_normal(secondary_key, -3.0, 3.0, (2, ANTENNA_NUMBER, ANTENNA_NUMBER), jnp.float32)
    real_part = (baseline_level[0] + baseline_level[0].T) * 0.5
    imag_part = (baseline_level[1] - baseline_level[1].T) * 0.5
    outer = scales[:, None] * scales[None, :]
    return jnp.stack([real_part * outer, imag_part * outer], axis=1).astype(jnp.bfloat16)


def draw_initial_gains(key, part):
    primary_key, secondary_key = jax.random.split(jax.random.fold_in(key, 23))
    lower_limit = 0.5
    upper_limit = 2.0
    gain_amplitude = jnp.exp(jax.random.uniform(primary_key, (ANTENNA_NUMBER,), jnp.float32, math.log(lower_limit), math.log(upper_limit)))
    gain_phase = jax.random.uniform(secondary_key, (ANTENNA_NUMBER,), jnp.float32, -math.pi, math.pi)
    return jnp.stack([gain_amplitude * jnp.cos(gain_phase), gain_amplitude * jnp.sin(gain_phase)]).astype(jnp.float32)


def shard_levels(stream_key, dims, cuts, least, largest):
    loudness = 1.0
    for position, blocks in cuts:
        heights = jax.random.uniform(jax.random.fold_in(jax.random.fold_in(stream_key, 6), position), (blocks,), jnp.float32, least / len(cuts), largest / len(cuts))
        loudness = loudness * jnp.repeat(jnp.exp(heights), dims[position] // blocks).reshape((-1,) + (1,) * (len(dims) - 1 - position))
    return loudness


def gaussian(key, shape, deviation, most, pieces=(), kind=jnp.bfloat16):
    array = jax.random.normal(key, shape, jnp.float32) * deviation
    if len(pieces) > 0:
        array = shard_levels(key, shape, pieces, -0.22, 0.18) * array
    return jnp.clip(array, min=-most, max=most).astype(kind)


def setup_inputs(seed: int = 0, part: int = 0) -> dict:
    streams_of = jax.random.split(jax.random.key(seed), 4)
    part_keys = jax.random.split(jax.random.fold_in(streams_of[3], part), 4)
    return {
        "samples": gaussian(part_keys[0], (ANTENNA_NUMBER, 2, TIME_SAMPLES), 1.0, 6.0, ((0, 8), (2, 16))),
        "sky_model": draw_sky_model(jax.random.fold_in(jax.random.fold_in(streams_of[3], part), 71), part),
        "initial_gains": draw_initial_gains(jax.random.fold_in(jax.random.fold_in(streams_of[3], part), 71), part),
    }


def reference(samples, sky_model, initial_gains):
    antennas = samples.shape[0]
    flattened = samples.reshape(antennas, -1)
    rotated = jnp.concatenate([-samples[:, 1, :], samples[:, 0, :]], axis=1)
    vis_real = jnp.dot(flattened, flattened.T, preferred_element_type=jnp.float32)
    vis_imag = jnp.dot(flattened, rotated.T, preferred_element_type=jnp.float32)
    model_real = sky_model[:, 0, :].astype(jnp.float32)
    model_imag = sky_model[:, 1, :].astype(jnp.float32)
    cross_mask = 1.0 - jnp.eye(antennas, dtype=jnp.float32)
    weight_real = (vis_real * model_real + vis_imag * model_imag) * cross_mask
    weight_imag = (vis_real * model_imag - vis_imag * model_real) * cross_mask
    model_power = (model_real * model_real + model_imag * model_imag) * cross_mask
    upper_limit = lax.Precision.HIGHEST
    gain_real = initial_gains[0]
    gain_imag = initial_gains[1]
    for iteration in range(ITERS):
        numer_real = jnp.dot(gain_real, weight_real, precision=upper_limit) - jnp.dot(gain_imag, weight_imag, precision=upper_limit)
        numer_imag = jnp.dot(gain_imag, weight_real, precision=upper_limit) + jnp.dot(gain_real, weight_imag, precision=upper_limit)
        energy = jnp.dot(gain_real * gain_real + gain_imag * gain_imag, model_power, precision=upper_limit)
        new_real = numer_real / energy
        new_imag = numer_imag / energy
        if iteration == 1:
            new_real = 0.5 * (new_real + gain_real)
            new_imag = 0.5 * (new_imag + gain_imag)
        gain_real = new_real
        gain_imag = new_imag
    return jnp.stack([gain_real, gain_imag])
```

```python
import jax
import jax.numpy as jnp
from jax import lax
from jax.sharding import PartitionSpec as P


def vis_tiles(samples):
    block_column = samples.shape[0]
    flattened = samples.reshape(block_column, -1)
    rotated = jnp.concatenate([-samples[:, 1, :], samples[:, 0, :]], axis=1)
    right_side = jnp.concatenate([flattened, rotated], axis=0)
    all_antennas = lax.all_gather(flattened, "col", axis=0, tiled=True)
    vis_tile = lax.psum_scatter(
        lax.dot_general(
            all_antennas, right_side, (((1,), (1,)), ((), ())), preferred_element_type=jnp.float32
        ),
        "row",
        scatter_dimension=0,
        tiled=True,
    )
    return vis_tile[:, :block_column], vis_tile[:, block_column:]


def exchange(parts, axis):
    count = lax.axis_size(axis)
    copies = jnp.broadcast_to(parts[None], (count,) + parts.shape)
    return lax.all_to_all(copies, axis, 0, 0)


def columns_to_rows(weight_real, weight_imag, power, gain):
    real = gain[0][None, :]
    imag = gain[1][None, :]
    return jnp.stack(
        [
            jnp.sum(weight_real * real + weight_imag * imag, axis=1),
            jnp.sum(weight_real * imag - weight_imag * real, axis=1),
            jnp.sum(power * (real * real + imag * imag), axis=1),
        ]
    )


def rows_to_columns(weight_real, weight_imag, power, gain):
    real = gain[0][:, None]
    imag = gain[1][:, None]
    return jnp.stack(
        [
            jnp.sum(weight_real * real - weight_imag * imag, axis=0),
            jnp.sum(weight_real * imag + weight_imag * real, axis=0),
            jnp.sum(power * (real * real + imag * imag), axis=0),
        ]
    )


def body(samples, sky_model, initial_gains):
    row_count = lax.axis_size("row")
    column_count = lax.axis_size("col")
    row_index = lax.axis_index("row")
    column_index = lax.axis_index("col")
    block_column = samples.shape[0]
    block_row = sky_model.shape[0]
    share_size = initial_gains.shape[1]
    blocks = block_column // block_row
    everything = lax.all_gather(initial_gains, ("row", "col"), axis=1, tiled=True)
    gain = lax.dynamic_slice_in_dim(everything, column_index * block_column, block_column, 1)
    vis_real, vis_imag = vis_tiles(samples)
    model_real = sky_model[:, 0, :].astype(jnp.float32)
    model_imag = sky_model[:, 1, :].astype(jnp.float32)
    global_rows = row_index * block_row + lax.broadcasted_iota(
        jnp.int32, (block_row, block_column), 0
    )
    global_columns = column_index * block_column + lax.broadcasted_iota(
        jnp.int32, (block_row, block_column), 1
    )
    cross_mask = (global_rows != global_columns).astype(jnp.float32)
    weight_real = (vis_real * model_real + vis_imag * model_imag) * cross_mask
    weight_imag = (vis_real * model_imag - vis_imag * model_real) * cross_mask
    power = (model_real * model_real + model_imag * model_imag) * cross_mask

    parts = columns_to_rows(weight_real, weight_imag, power, gain)
    sums = jnp.sum(exchange(parts, "col"), axis=0)
    gain = sums[:2] / sums[2:]

    parts = rows_to_columns(weight_real, weight_imag, power, gain)
    message = jnp.concatenate([parts.reshape(-1), gain.reshape(-1)])
    message = message.reshape(-1, 128)
    received = exchange(message, "row").reshape(row_count, -1)
    sums = jnp.sum(received[:, : 3 * block_column], axis=0).reshape(3, block_column)
    previous = lax.dynamic_slice_in_dim(
        received[:, 3 * block_column :], column_index * blocks, blocks, 0
    )
    previous = previous.reshape(blocks, 2, block_row).transpose(1, 0, 2).reshape(2, block_column)
    gain = 0.5 * (sums[:2] / sums[2:] + previous)

    parts = columns_to_rows(weight_real, weight_imag, power, gain)
    shares = parts.reshape(3, column_count, share_size).transpose(1, 0, 2)
    sums = jnp.sum(lax.all_to_all(shares, "col", 0, 0), axis=0)
    return sums[:2] / sums[2:]


def solution(mesh):
    return jax.shard_map(
        body,
        mesh=mesh,
        in_specs=(
            P(("chan", "col"), None, "row"),
            P(("chan", "row"), None, "col"),
            P(None, ("chan", "row", "col")),
        ),
        out_specs=P(None, ("chan", "row", "col")),
        check_vma=False,
    )
```

```python
import functools

import jax
import jax.numpy as jnp
import numpy as np
from jax import lax
from jax.experimental import pallas as pl
from jax.experimental.pallas import tpu as pltpu
from jax.sharding import PartitionSpec as P


SIDE = 4
PLANES = 8

OFFSETS = {0: (0, 0), 1: (0, 1), 2: (-1, 1), 3: (-1, 2), 4: (-2, 2)}
EARLY = [(d, h, k) for d in (1, 2) for h in (0, 1) for k in (0, 1)]
LATE = [(3, h, k) for h in (0, 1) for k in (0, 1)] + [(4, 0, 0), (4, 1, 1), (0, 0, 0), (0, 0, 1)]
PLACE = [
    [7, 0, 2, 5, 13, 10, 8, 15, 14, 6, 3, 12, 11, 9, 1, 4],
    [15, 10, 8, 2, 0, 7, 5, 13, 9, 4, 1, 14, 6, 11, 12, 3],
    [13, 8, 5, 10, 2, 0, 7, 15, 11, 14, 3, 1, 12, 9, 6, 4],
    [10, 13, 15, 2, 0, 8, 7, 5, 11, 4, 14, 9, 1, 12, 3, 6],
    [15, 8, 13, 10, 2, 5, 7, 0, 11, 6, 4, 14, 3, 1, 12, 9],
    [2, 10, 15, 0, 8, 5, 7, 13, 11, 12, 14, 9, 3, 1, 6, 4],
    [15, 0, 2, 13, 5, 8, 10, 7, 9, 14, 3, 11, 6, 4, 1, 12],
    [2, 5, 7, 10, 8, 0, 15, 13, 3, 12, 9, 1, 4, 6, 11, 14],
]


def targets(chunk, c):
    d, h, k = chunk
    a, b = [(c + offset) % PLANES for offset in OFFSETS[d]]
    if d == 0 and k == 0:
        return (2 * c, c, 0), (2 * c + 1, c, 1), 0
    if d == 0:
        return (2 * c + 1, c, 0), (2 * c, c, 1), 1
    if d == 4:
        k = h if c < PLANES // 2 else 1 - h
    plain, mirror = (2 * a + h, b, k), (2 * b + k, a, h)
    if d == 4 or h == k:
        return plain, mirror, 0
    return mirror, plain, 1


def tables():
    rows = SIDE * SIDE
    first, second = [], []
    flip = np.zeros((rows, PLANES), np.int32)
    diagonal = np.zeros((rows, PLANES), np.int32)
    half = np.zeros((rows, PLANES), np.int32)
    for c in range(PLANES):
        for chunk, r in zip(EARLY + LATE, PLACE[c]):
            one, two, conjugated = targets(chunk, c)
            first.append((r * PLANES + c, one[0] * PLANES + one[1]))
            second.append((r * PLANES + c, two[0] * PLANES + two[1]))
            flip[r, c] = conjugated
            diagonal[r, c] = chunk == (0, 0, 0)
            half[one[0], one[1]] = one[2]
    return first, second, flip, diagonal, half


def slots():
    place = np.array(PLACE, np.int32)
    y, x = place // SIDE, place % SIDE
    table = np.stack([x, y // 2, y, x // 2], axis=-1)
    return table[:, :8].reshape(PLANES, -1), table[:, 8:].reshape(PLANES, -1)


def matmul(lhs, rhs):
    return lax.dot_general(lhs, rhs, (((1,), (1,)), ((), ())), preferred_element_type=jnp.float32)


def correlate(lhs, rhs):
    times = lhs.shape[1] // 2
    real = matmul(lhs, rhs)
    imag = matmul(lhs[:, times:], rhs[:, :times]) - matmul(lhs[:, :times], rhs[:, times:])
    return real, imag


def early_kernel(slot, here, above, below, real_out, imag_out):
    quarter = here.shape[0] // 2
    for i, (d, h, k) in enumerate(EARLY):
        lhs = here if d == 1 else below
        real, imag = correlate(
            lhs[h * quarter : (h + 1) * quarter, :], above[k * quarter : (k + 1) * quarter, :]
        )
        real_out[slot[4 * i], slot[4 * i + 1]] = real
        imag_out[slot[4 * i + 2], slot[4 * i + 3]] = imag


def late_kernel(slot, here, below, above2, below2, real_out, imag_out):
    quarter = here.shape[0] // 2
    for i, (d, h, k) in enumerate(LATE):
        low = slice(h * quarter, (h + 1) * quarter)
        if d == 3:
            real, imag = correlate(below[low, :], above2[k * quarter : (k + 1) * quarter, :])
        elif d == 4:
            other = pl.multiple_of((h ^ slot[4 * len(LATE)]) * quarter, quarter)
            real, imag = correlate(below2[low, :], above2[pl.ds(other, quarter), :])
        elif k == 1:
            real, imag = correlate(here[:quarter, :], here[quarter:, :])
        else:
            real = sum(correlate(here[:quarter, :], here[:quarter, :]))
            imag = sum(correlate(here[quarter:, :], here[quarter:, :]))
        real_out[slot[4 * i], slot[4 * i + 1]] = real
        imag_out[slot[4 * i + 2], slot[4 * i + 3]] = imag


def chunks(kernel, slot, blocks, products):
    antennas, samples = blocks[0].shape
    quarter = antennas // 2
    shape = jax.ShapeDtypeStruct((SIDE, 2, quarter, quarter), jnp.float32)
    vmem = pl.BlockSpec(memory_space=pltpu.VMEM)
    return pl.pallas_call(
        kernel,
        out_shape=(shape, shape),
        in_specs=[pl.BlockSpec(memory_space=pltpu.SMEM)] + [vmem] * len(blocks),
        out_specs=(vmem, vmem),
        cost_estimate=pl.CostEstimate(
            flops=products * 4 * quarter * quarter * samples,
            bytes_accessed=len(blocks) * antennas * samples * 2 + 64 * quarter * quarter,
            transcendentals=0,
        ),
    )(slot, *blocks)


def mirror_kernel(flags, real, imag, first, second):
    p, q = real[...], imag[...]
    pt, qt = p.T, q.T
    diagonal = flags[1] == 1
    flip = flags[0] == 1
    first[0] = jnp.where(diagonal, 0.5 * (p + pt), jnp.where(flip, pt, p))
    first[1] = jnp.where(diagonal, 0.5 * (p - pt), jnp.where(flip, -qt, q))
    second[0] = jnp.where(diagonal, 0.5 * (q + qt), jnp.where(flip, p, pt))
    second[1] = jnp.where(diagonal, 0.5 * (q - qt), jnp.where(flip, q, -qt))


def mirror(flags, real, imag):
    shape = jax.ShapeDtypeStruct((2,) + real.shape, jnp.float32)
    vmem = pl.BlockSpec(memory_space=pltpu.VMEM)
    return pl.pallas_call(
        mirror_kernel,
        out_shape=(shape, shape),
        in_specs=[pl.BlockSpec(memory_space=pltpu.SMEM), vmem, vmem],
        out_specs=(vmem, vmem),
    )(flags, real, imag)


def shift_x(value, step):
    pairs = [
        (y * SIDE + x, y * SIDE + (x + step) % SIDE) for y in range(SIDE) for x in range(SIDE)
    ]
    return lax.ppermute(value, "row", pairs)


def shift_y(value, step):
    pairs = [
        (y * SIDE + x, (y + step) % SIDE * SIDE + x) for y in range(SIDE) for x in range(SIDE)
    ]
    return lax.ppermute(value, "row", pairs)


def shift_z(value, step):
    return lax.ppermute(value, "col", [(c, (c + step) % PLANES) for c in range(PLANES)])


def ring_sums(rings):
    def entry(array, place, step):
        return lax.dynamic_index_in_dim(array, (place + step) % SIDE, 0, keepdims=False)

    far = []
    for shift, place, array in rings:
        opposite = entry(array, place, 2)
        far.append((shift(opposite[0], 1), shift(opposite[1], -1)))
    near = []
    for (shift, place, array), (from_left, from_right) in zip(rings, far):
        up, down = entry(array, place, 1), entry(array, place, 3)
        up = jnp.stack([up[0] + from_left, up[1]])
        down = jnp.stack([down[0], down[1] + from_right])
        near.append((entry(array, place, 0), shift(up, 1), shift(down, -1)))
    return [own + left + right for own, left, right in near]


def exchange(parts, axis):
    count = lax.axis_size(axis)
    copies = jnp.broadcast_to(parts[None], (count,) + parts.shape)
    return lax.all_to_all(copies, axis, 0, 0)


def columns_to_rows(weight_real, weight_imag, power, gain):
    real = gain[0][None, :]
    imag = gain[1][None, :]
    return jnp.stack(
        [
            jnp.sum(weight_real * real + weight_imag * imag, axis=1),
            jnp.sum(weight_real * imag - weight_imag * real, axis=1),
            jnp.sum(power * (real * real + imag * imag), axis=1),
        ]
    )


def rows_to_columns(weight_real, weight_imag, power, gain):
    real = gain[0][:, None]
    imag = gain[1][:, None]
    return jnp.stack(
        [
            jnp.sum(weight_real * real - weight_imag * imag, axis=0),
            jnp.sum(weight_real * imag + weight_imag * real, axis=0),
            jnp.sum(power * (real * real + imag * imag), axis=0),
        ]
    )


def vis_tiles(samples):
    row_index = lax.axis_index("row")
    column_index = lax.axis_index("col")
    y, x = row_index // SIDE, row_index % SIDE
    first, second, flip, diagonal, half = tables()
    early_slots, late_slots = slots()
    here = samples.reshape(samples.shape[0], -1)
    above, below = shift_z(here, -1), shift_z(here, 1)
    above2, below2 = shift_z(above, -1), shift_z(below, 1)
    early_real, early_imag = chunks(
        early_kernel, jnp.asarray(early_slots)[column_index], (here, above, below), 8
    )
    late_slot = jnp.concatenate(
        [
            jnp.asarray(late_slots)[column_index],
            (column_index >= PLANES // 2).astype(jnp.int32)[None],
        ]
    )
    early_sums = ring_sums([(shift_x, x, early_real), (shift_y, y, early_imag)])
    late_real, late_imag = chunks(late_kernel, late_slot, (here, below, above2, below2), 9)
    late_sums = ring_sums([(shift_x, x, late_real), (shift_y, y, late_imag)])
    rings = []
    for shift, place, fixed, early, late in (
        (shift_y, y, x, early_sums[0], late_sums[0]),
        (shift_x, x, y, early_sums[1], late_sums[1]),
    ):
        odd = fixed % 2 == 1
        pairs = jnp.stack([jnp.where(odd, late, early), jnp.where(odd, early, late)], axis=1)
        quarter = early.shape[-1]
        rings.append((shift, place, pairs.reshape(SIDE, 2, quarter // 2, quarter)))
    real, imag = [value.reshape(quarter, quarter) for value in ring_sums(rings)]
    flags = jnp.stack(
        [
            jnp.asarray(flip)[row_index, column_index],
            jnp.asarray(diagonal)[row_index, column_index],
        ]
    )
    one, two = mirror(flags, real, imag)
    one = lax.ppermute(one, ("row", "col"), first)
    two = lax.ppermute(two, ("row", "col"), second)
    one_is_right = jnp.asarray(half)[row_index, column_index] == 1
    left = jnp.where(one_is_right, two, one)
    right = jnp.where(one_is_right, one, two)
    return jnp.concatenate([left[0], right[0]], axis=1), jnp.concatenate([left[1], right[1]], axis=1)


def body(samples, sky_model, initial_gains):
    row_count = lax.axis_size("row")
    column_count = lax.axis_size("col")
    row_index = lax.axis_index("row")
    column_index = lax.axis_index("col")
    block_column = samples.shape[0]
    block_row = sky_model.shape[0]
    share_size = initial_gains.shape[1]
    blocks = block_column // block_row
    row_gains = lax.all_gather(initial_gains, "col", axis=1, tiled=True)
    gain = lax.dynamic_slice_in_dim(
        exchange(row_gains, "row"), column_index * blocks, blocks, 0
    )
    gain = gain.transpose(1, 0, 2).reshape(2, block_column)
    vis_real, vis_imag = vis_tiles(samples)
    model_real = sky_model[:, 0, :].astype(jnp.float32)
    model_imag = sky_model[:, 1, :].astype(jnp.float32)
    global_rows = row_index * block_row + lax.broadcasted_iota(
        jnp.int32, (block_row, block_column), 0
    )
    global_columns = column_index * block_column + lax.broadcasted_iota(
        jnp.int32, (block_row, block_column), 1
    )
    cross_mask = (global_rows != global_columns).astype(jnp.float32)
    weight_real = (vis_real * model_real + vis_imag * model_imag) * cross_mask
    weight_imag = (vis_real * model_imag - vis_imag * model_real) * cross_mask
    power = (model_real * model_real + model_imag * model_imag) * cross_mask

    parts = columns_to_rows(weight_real, weight_imag, power, gain)
    sums = jnp.sum(exchange(parts, "col"), axis=0)
    gain = sums[:2] / sums[2:]

    parts = rows_to_columns(weight_real, weight_imag, power, gain)
    message = jnp.concatenate([parts.reshape(-1), gain.reshape(-1)])
    message = message.reshape(-1, 128)
    received = exchange(message, "row").reshape(row_count, -1)
    sums = jnp.sum(received[:, : 3 * block_column], axis=0).reshape(3, block_column)
    previous = lax.dynamic_slice_in_dim(
        received[:, 3 * block_column :], column_index * blocks, blocks, 0
    )
    previous = previous.reshape(blocks, 2, block_row).transpose(1, 0, 2).reshape(2, block_column)
    gain = 0.5 * (sums[:2] / sums[2:] + previous)

    parts = columns_to_rows(weight_real, weight_imag, power, gain)
    shares = parts.reshape(3, column_count, share_size).transpose(1, 0, 2)
    sums = jnp.sum(lax.all_to_all(shares, "col", 0, 0), axis=0)
    return sums[:2] / sums[2:]


def solution(mesh):
    return jax.shard_map(
        body,
        mesh=mesh,
        in_specs=(
            P(("chan", "col"), None, "row"),
            P(("chan", "row"), None, "col"),
            P(None, ("chan", "row", "col")),
        ),
        out_specs=P(None, ("chan", "row", "col")),
        check_vma=False,
    )
```

```python
import jax
import jax.numpy as jnp
import numpy as np
from jax import lax
from jax.experimental import pallas as pl
from jax.experimental.pallas import tpu as pltpu
from jax.sharding import PartitionSpec as P


SIDE = 4
PLANES = 8

OFFSETS = {0: (0, 0), 1: (0, 1), 2: (-1, 1), 3: (-1, 2), 4: (-2, 2)}
EARLY = [(d, h, k) for d in (1, 2) for h in (0, 1) for k in (0, 1)]
LATE = [(3, h, k) for h in (0, 1) for k in (0, 1)] + [(4, 0, 0), (4, 1, 1), (0, 0, 0), (0, 0, 1)]
PLACE = [
    [7, 0, 2, 5, 13, 10, 8, 15, 14, 6, 3, 12, 11, 9, 1, 4],
    [15, 10, 8, 2, 0, 7, 5, 13, 9, 4, 1, 14, 6, 11, 12, 3],
    [13, 8, 5, 10, 2, 0, 7, 15, 11, 14, 3, 1, 12, 9, 6, 4],
    [10, 13, 15, 2, 0, 8, 7, 5, 11, 4, 14, 9, 1, 12, 3, 6],
    [15, 8, 13, 10, 2, 5, 7, 0, 11, 6, 4, 14, 3, 1, 12, 9],
    [2, 10, 15, 0, 8, 5, 7, 13, 11, 12, 14, 9, 3, 1, 6, 4],
    [15, 0, 2, 13, 5, 8, 10, 7, 9, 14, 3, 11, 6, 4, 1, 12],
    [2, 5, 7, 10, 8, 0, 15, 13, 3, 12, 9, 1, 4, 6, 11, 14],
]


def targets(chunk, c):
    d, h, k = chunk
    a, b = [(c + offset) % PLANES for offset in OFFSETS[d]]
    if d == 0 and k == 0:
        return (2 * c, c, 0), (2 * c + 1, c, 1), 0
    if d == 0:
        return (2 * c + 1, c, 0), (2 * c, c, 1), 1
    if d == 4:
        k = h if c < PLANES // 2 else 1 - h
    plain, mirror = (2 * a + h, b, k), (2 * b + k, a, h)
    if d == 4 or h == k:
        return plain, mirror, 0
    return mirror, plain, 1


def tables():
    rows = SIDE * SIDE
    devices = rows * PLANES
    first, second = [], []
    early = np.zeros((devices, 2, SIDE, 2), np.int32)
    late = np.zeros((devices, 2, SIDE, 2), np.int32)
    ahead = np.zeros((devices, 2, SIDE), np.int32)
    flags = np.zeros((devices, 2), np.int32)
    half = np.zeros(devices, np.int32)
    for c in range(PLANES):
        for chunk, r in zip(EARLY + LATE, PLACE[c]):
            one, two, conjugated = targets(chunk, c)
            first.append((r * PLANES + c, one[0] * PLANES + one[1]))
            second.append((r * PLANES + c, two[0] * PLANES + two[1]))
            flags[r * PLANES + c] = conjugated, chunk == (0, 0, 0)
            half[one[0] * PLANES + one[1]] = one[2]
        for i, owner in enumerate(PLACE[c]):
            v, u = owner // SIDE, owner % SIDE
            order, index = (early, i) if i < len(EARLY) else (late, i - len(EARLY))
            for r in range(rows):
                y, x = r // SIDE, r % SIDE
                order[r * PLANES + c, 0, (u - x) % SIDE, v // 2] = index
                order[r * PLANES + c, 1, (v - y) % SIDE, u // 2] = index
        for r in range(rows):
            y, x = r // SIDE, r % SIDE
            for t in range(SIDE):
                v, u = (y + t) % SIDE, (x + t) % SIDE
                ahead[r * PLANES + c, 0, t] = (v + x) % 2 * 2 + v // 2
                ahead[r * PLANES + c, 1, t] = (u + y) % 2 * 2 + u // 2
    return first, second, early, late, ahead, flags, half


def matmul(lhs, rhs):
    return lax.dot_general(lhs, rhs, (((1,), (1,)), ((), ())), preferred_element_type=jnp.float32)


def real_part(lhs, rhs):
    return matmul(lhs, rhs)


def imag_part(lhs, rhs):
    times = lhs.shape[1] // 2
    return matmul(lhs[:, times:], rhs[:, :times]) - matmul(lhs[:, :times], rhs[:, times:])


def diagonal_kernel(here, out):
    quarter = here.shape[0] // 2

    @pl.loop(0, 3)
    def _(i):
        low = pl.ds(pl.multiple_of(jnp.where(i == 1, quarter, 0), quarter), quarter)
        other = pl.ds(pl.multiple_of(jnp.where(i == 0, 0, quarter), quarter), quarter)
        lhs, rhs = here[low, :], here[other, :]
        out[2 * i] = real_part(lhs, rhs)
        out[2 * i + 1] = imag_part(lhs, rhs)


def stores(right, left, up, down, own):
    return {
        (0, 0): own.at[0],
        (0, 1): own.at[1],
        (1, 0): up,
        (1, 1): right.at[1],
        (2, 0): right.at[0],
        (2, 1): left.at[0],
        (3, 0): left.at[1],
        (3, 1): down,
    }


ORDER = ((2, 0), (1, 1), (2, 1), (3, 0), (1, 0), (3, 1), (0, 0), (0, 1))


def early_kernel(device, table, here, above, below, *outs):
    quarter = here.shape[0] // 2
    for t, j in ORDER:
        for color, part in enumerate((real_part, imag_part)):
            index = table[device[0] * 16 + color * 8 + t * 2 + j]
            low = pl.ds(pl.multiple_of((index // 2 % 2) * quarter, quarter), quarter)
            other = pl.ds(pl.multiple_of((index % 2) * quarter, quarter), quarter)
            lhs = jnp.where(index < 4, here[low, :], below[low, :])
            stores(*outs[5 * color : 5 * color + 5])[t, j][...] = part(lhs, above[other, :])


def late_kernel(device, table, diagonal, below, above2, below2, *refs):
    outs, found = refs[:-1], refs[-1]
    quarter = below.shape[0] // 2
    upper = (device[1] >= PLANES // 2).astype(jnp.int32)

    @pl.loop(0, 2 * SIDE)
    def _(place):
        for color, part in enumerate((real_part, imag_part)):
            index = table[device[0] * 16 + color * 8 + place]
            out = found.at[color * 8 + place]

            @pl.when(index < 6)
            def _():
                near = index < 4
                h = jnp.where(near, index // 2, index - 4)
                k = jnp.where(near, index % 2, (h + upper) % 2)
                low = pl.ds(pl.multiple_of(h * quarter, quarter), quarter)
                other = pl.ds(pl.multiple_of(k * quarter, quarter), quarter)
                lhs = jnp.where(near, below[low, :], below2[low, :])
                out[...] = part(lhs, above2[other, :])

            @pl.when(index >= 6)
            def _():
                packed = diagonal[2 * color] + diagonal[2 * color + 1]
                out[...] = jnp.where(index == 6, packed, diagonal[4 + color])

    for color in range(2):
        places = stores(*outs[5 * color : 5 * color + 5])
        for t, j in ORDER:
            places[t, j][...] = found[color * 8 + t * 2 + j]


def finish_kernel(device, ahead, *refs):
    ins, outs, sums = refs[:20], refs[20:30], refs[30]
    quarter = sums.shape[-1]
    half = quarter // 2
    for color in range(2):
        for group in range(2):
            own, right, left, right2, left2 = ins[10 * color + 5 * group :][:5]
            sums[2 * group] = own[0] + right2[...] + left[1]
            sums[2 * group + 1] = own[1] + right[1] + left2[...]
        right, left, up, down, own = outs[5 * color : 5 * color + 5]
        entry = [sums.at[ahead[device[0] * 8 + color * 4 + t]] for t in range(SIDE)]
        own[...] = entry[0][...]
        up[...] = entry[1][:half, :]
        right[1] = entry[1][half:, :]
        right[0] = entry[2][:half, :]
        left[0] = entry[2][half:, :]
        left[1] = entry[3][:half, :]
        down[...] = entry[3][half:, :]


def mirror_kernel(device, flags, *refs):
    total = []
    for own, right, left, right2, left2 in (refs[:5], refs[5:10]):
        half = right2.shape[0]
        total.append(
            jnp.concatenate(
                [
                    own[:half, :] + right2[...] + left[1],
                    own[half:, :] + right[1] + left2[...],
                ]
            )
        )
    first, second = refs[10:]
    p, q = total
    pt, qt = p.T, q.T
    flip = flags[device[0] * 2] == 1
    diagonal = flags[device[0] * 2 + 1] == 1
    first[0] = jnp.where(diagonal, 0.5 * (p + pt), jnp.where(flip, pt, p))
    first[1] = jnp.where(diagonal, 0.5 * (p - pt), jnp.where(flip, -qt, q))
    second[0] = jnp.where(diagonal, 0.5 * (q + qt), jnp.where(flip, p, pt))
    second[1] = jnp.where(diagonal, 0.5 * (q - qt), jnp.where(flip, q, -qt))


def kernel_call(kernel, scalars, blocks, shapes, flops=0, scratch=()):
    shapes = [jax.ShapeDtypeStruct(shape, jnp.float32) for shape in shapes]
    vmem = pl.BlockSpec(memory_space=pltpu.VMEM)
    smem = pl.BlockSpec(memory_space=pltpu.SMEM)
    moved = sum(v.size * v.dtype.itemsize for v in blocks) + sum(4 * v.size for v in shapes)
    return pl.pallas_call(
        kernel,
        out_shape=shapes,
        in_specs=[smem] * len(scalars) + [vmem] * len(blocks),
        out_specs=[vmem] * len(shapes),
        scratch_shapes=scratch,
        cost_estimate=pl.CostEstimate(flops=flops, bytes_accessed=moved, transcendentals=0),
    )(*scalars, *blocks)


def message_shapes(rows, columns):
    return [(2, rows, columns)] * 2 + [(rows, columns)] * 2


def shift_x(value, step):
    pairs = [
        (y * SIDE + x, y * SIDE + (x + step) % SIDE) for y in range(SIDE) for x in range(SIDE)
    ]
    return lax.ppermute(value, "row", pairs)


def shift_y(value, step):
    pairs = [
        (y * SIDE + x, (y + step) % SIDE * SIDE + x) for y in range(SIDE) for x in range(SIDE)
    ]
    return lax.ppermute(value, "row", pairs)


def shift_z(value, step):
    return lax.ppermute(value, "col", [(c, (c + step) % PLANES) for c in range(PLANES)])


def ring_start(outs, shift):
    right, left, up, down, own = outs
    right, left = shift(right, 1), shift(left, -1)
    return own, right, left, up + right[0], down + left[0]


def ring_end(parts, shift):
    own, right, left, up, down = parts
    return own, right, left, shift(up, 1), shift(down, -1)


def ring(outs, shift):
    return ring_end(ring_start(outs, shift), shift)


def exchange(parts, axis):
    count = lax.axis_size(axis)
    copies = jnp.broadcast_to(parts[None], (count,) + parts.shape)
    return lax.all_to_all(copies, axis, 0, 0)


def columns_to_rows(weight_real, weight_imag, power, gain):
    real = gain[0][None, :]
    imag = gain[1][None, :]
    return jnp.stack(
        [
            jnp.sum(weight_real * real + weight_imag * imag, axis=1),
            jnp.sum(weight_real * imag - weight_imag * real, axis=1),
            jnp.sum(power * (real * real + imag * imag), axis=1),
        ]
    )


def rows_to_columns(weight_real, weight_imag, power, gain):
    real = gain[0][:, None]
    imag = gain[1][:, None]
    return jnp.stack(
        [
            jnp.sum(weight_real * real - weight_imag * imag, axis=0),
            jnp.sum(weight_real * imag + weight_imag * real, axis=0),
            jnp.sum(power * (real * real + imag * imag), axis=0),
        ]
    )


def vis_tiles(samples, gain):
    row_index = lax.axis_index("row")
    column_index = lax.axis_index("col")
    first, second, early, late, ahead, flags, half = tables()
    device_index = row_index * PLANES + column_index
    device = jnp.stack([device_index, column_index]).astype(jnp.int32)
    here = samples.reshape(samples.shape[0], -1)
    antennas, times = here.shape
    quarter = antennas // 2
    product = 2 * quarter * quarter * times
    above, below = shift_z(here, -1), shift_z(here, 1)
    gain, free = lax.optimization_barrier((gain, here))
    (diagonal,) = kernel_call(diagonal_kernel, (), (free,), [(6, quarter, quarter)], 6 * product)
    above, below, diagonal = lax.optimization_barrier((above, below, diagonal))
    above2, below2 = shift_z(above, -1), shift_z(below, 1)
    shapes = 2 * (message_shapes(quarter, quarter) + [(2, quarter, quarter)])
    outs = kernel_call(
        early_kernel,
        (device, jnp.asarray(early.reshape(-1))),
        (here, above, below),
        shapes,
        16 * product,
    )
    along_x, along_y = ring_start(outs[:5], shift_x), ring_start(outs[5:], shift_y)
    sums = along_x[3:] + along_y[3:]
    *_, above2, below2 = lax.optimization_barrier((*sums, above2, below2))
    early_parts = ring_end(along_x, shift_x), ring_end(along_y, shift_y)
    outs = kernel_call(
        late_kernel,
        (device, jnp.asarray(late.reshape(-1))),
        (diagonal, below, above2, below2),
        shapes,
        12 * product,
        scratch=(pltpu.VMEM((16, quarter, quarter), jnp.float32),),
    )
    late_parts = ring(outs[:5], shift_x), ring(outs[5:], shift_y)
    outs = kernel_call(
        finish_kernel,
        (device, jnp.asarray(ahead.reshape(-1))),
        early_parts[0] + late_parts[0] + early_parts[1] + late_parts[1],
        2 * (message_shapes(quarter // 2, quarter) + [(quarter, quarter)]),
        scratch=(pltpu.VMEM((4, quarter, quarter), jnp.float32),),
    )
    parts = ring(outs[:5], shift_y) + ring(outs[5:], shift_x)
    one, two = kernel_call(
        mirror_kernel,
        (device, jnp.asarray(flags.reshape(-1))),
        parts,
        [(2, quarter, quarter)] * 2,
    )
    one = lax.ppermute(one, ("row", "col"), first)
    two = lax.ppermute(two, ("row", "col"), second)
    one_is_right = jnp.asarray(half)[device_index] == 1
    left = jnp.where(one_is_right, two, one)
    right = jnp.where(one_is_right, one, two)
    real = jnp.concatenate([left[0], right[0]], axis=1)
    imag = jnp.concatenate([left[1], right[1]], axis=1)
    return real, imag, gain


def starting_gains(initial_gains):
    blocks = SIDE * SIDE // PLANES
    pairs = [
        (r * PLANES + c, (r % blocks * PLANES + c) * PLANES + r // blocks)
        for r in range(SIDE * SIDE)
        for c in range(PLANES)
    ]
    share = lax.ppermute(initial_gains, ("row", "col"), pairs)
    return exchange(share, "row").transpose(1, 0, 2).reshape(2, -1)


def body(samples, sky_model, initial_gains):
    row_count = lax.axis_size("row")
    column_count = lax.axis_size("col")
    row_index = lax.axis_index("row")
    column_index = lax.axis_index("col")
    block_column = samples.shape[0]
    block_row = sky_model.shape[0]
    share_size = initial_gains.shape[1]
    blocks = block_column // block_row
    gain = starting_gains(initial_gains)
    vis_real, vis_imag, gain = vis_tiles(samples, gain)
    model_real = sky_model[:, 0, :].astype(jnp.float32)
    model_imag = sky_model[:, 1, :].astype(jnp.float32)
    global_rows = row_index * block_row + lax.broadcasted_iota(
        jnp.int32, (block_row, block_column), 0
    )
    global_columns = column_index * block_column + lax.broadcasted_iota(
        jnp.int32, (block_row, block_column), 1
    )
    cross_mask = (global_rows != global_columns).astype(jnp.float32)
    weight_real = (vis_real * model_real + vis_imag * model_imag) * cross_mask
    weight_imag = (vis_real * model_imag - vis_imag * model_real) * cross_mask
    power = (model_real * model_real + model_imag * model_imag) * cross_mask

    parts = columns_to_rows(weight_real, weight_imag, power, gain)
    sums = jnp.sum(exchange(parts, "col"), axis=0)
    gain = sums[:2] / sums[2:]

    parts = rows_to_columns(weight_real, weight_imag, power, gain)
    message = jnp.concatenate([parts.reshape(-1), gain.reshape(-1)])
    message = message.reshape(-1, 128)
    received = exchange(message, "row").reshape(row_count, -1)
    sums = jnp.sum(received[:, : 3 * block_column], axis=0).reshape(3, block_column)
    previous = lax.dynamic_slice_in_dim(
        received[:, 3 * block_column :], column_index * blocks, blocks, 0
    )
    previous = previous.reshape(blocks, 2, block_row).transpose(1, 0, 2).reshape(2, block_column)
    gain = 0.5 * (sums[:2] / sums[2:] + previous)

    parts = columns_to_rows(weight_real, weight_imag, power, gain)
    shares = parts.reshape(3, column_count, share_size).transpose(1, 0, 2)
    sums = jnp.sum(lax.all_to_all(shares, "col", 0, 0), axis=0)
    return sums[:2] / sums[2:]


def solution(mesh):
    return jax.shard_map(
        body,
        mesh=mesh,
        in_specs=(
            P(("chan", "col"), None, "row"),
            P(("chan", "row"), None, "col"),
            P(None, ("chan", "row", "col")),
        ),
        out_specs=P(None, ("chan", "row", "col")),
        check_vma=False,
    )
```

```python
import jax
import jax.numpy as jnp
import numpy as np
from jax import lax
from jax.experimental import pallas as pl
from jax.experimental.pallas import tpu as pltpu
from jax.sharding import PartitionSpec as P


SIDE = 4
PLANES = 8

OFFSETS = {0: (0, 0), 1: (0, 1), 2: (-1, 1), 3: (-1, 2), 4: (-2, 2)}
EARLY = [(d, h, k) for d in (1, 2) for h in (0, 1) for k in (0, 1)]
LATE = [(3, h, k) for h in (0, 1) for k in (0, 1)] + [(4, 0, 0), (4, 1, 1), (0, 0, 0), (0, 0, 1)]
PLACE = [
    [7, 0, 2, 5, 13, 10, 8, 15, 14, 6, 3, 12, 11, 9, 1, 4],
    [15, 10, 8, 2, 0, 7, 5, 13, 9, 4, 1, 14, 6, 11, 12, 3],
    [13, 8, 5, 10, 2, 0, 7, 15, 11, 14, 3, 1, 12, 9, 6, 4],
    [10, 13, 15, 2, 0, 8, 7, 5, 11, 4, 14, 9, 1, 12, 3, 6],
    [15, 8, 13, 10, 2, 5, 7, 0, 11, 6, 4, 14, 3, 1, 12, 9],
    [2, 10, 15, 0, 8, 5, 7, 13, 11, 12, 14, 9, 3, 1, 6, 4],
    [15, 0, 2, 13, 5, 8, 10, 7, 9, 14, 3, 11, 6, 4, 1, 12],
    [2, 5, 7, 10, 8, 0, 15, 13, 3, 12, 9, 1, 4, 6, 11, 14],
]


def targets(chunk, c):
    d, h, k = chunk
    a, b = [(c + offset) % PLANES for offset in OFFSETS[d]]
    if d == 0 and k == 0:
        return (2 * c, c, 0), (2 * c + 1, c, 1), 0
    if d == 0:
        return (2 * c + 1, c, 0), (2 * c, c, 1), 1
    if d == 4:
        k = h if c < PLANES // 2 else 1 - h
    plain, mirror = (2 * a + h, b, k), (2 * b + k, a, h)
    if d == 4 or h == k:
        return plain, mirror, 0
    return mirror, plain, 1


def tables():
    rows = SIDE * SIDE
    devices = rows * PLANES
    first, second = [], []
    early = np.zeros((devices, 2, SIDE, 2), np.int32)
    late = np.zeros((devices, 2, SIDE, 2), np.int32)
    ahead = np.zeros((devices, 2, SIDE), np.int32)
    flags = np.zeros((devices, 2), np.int32)
    half = np.zeros(devices, np.int32)
    for c in range(PLANES):
        for chunk, r in zip(EARLY + LATE, PLACE[c]):
            one, two, conjugated = targets(chunk, c)
            first.append((r * PLANES + c, one[0] * PLANES + one[1]))
            second.append((r * PLANES + c, two[0] * PLANES + two[1]))
            flags[r * PLANES + c] = conjugated, chunk == (0, 0, 0)
            half[one[0] * PLANES + one[1]] = one[2]
        for i, owner in enumerate(PLACE[c]):
            v, u = owner // SIDE, owner % SIDE
            order, index = (early, i) if i < len(EARLY) else (late, i - len(EARLY))
            for r in range(rows):
                y, x = r // SIDE, r % SIDE
                order[r * PLANES + c, 0, (u - x) % SIDE, v // 2] = index
                order[r * PLANES + c, 1, (v - y) % SIDE, u // 2] = index
        for r in range(rows):
            y, x = r // SIDE, r % SIDE
            for t in range(SIDE):
                v, u = (y + t) % SIDE, (x + t) % SIDE
                ahead[r * PLANES + c, 0, t] = (v + x) % 2 * 2 + v // 2
                ahead[r * PLANES + c, 1, t] = (u + y) % 2 * 2 + u // 2
    return first, second, early, late, ahead, flags, half


def matmul(lhs, rhs):
    return lax.dot_general(lhs, rhs, (((1,), (1,)), ((), ())), preferred_element_type=jnp.float32)


def rows_of(ref, half):
    quarter = ref.shape[0] // 2
    return ref[pl.ds(pl.multiple_of(half * quarter, quarter), quarter), :]


def side_by_side(out, real, imag):
    times = real.shape[1]
    out[:, :times] = real[...]
    out[:, times:] = imag[...]


def turned(out, real, imag):
    times = real.shape[1]
    out[:, :times] = -imag[...]
    out[:, times:] = real[...]


def diagonal_kernel(real, imag, out, block, found):
    side_by_side(block.at[0], real, imag)
    turned(block.at[1], real, imag)

    @pl.loop(0, 6)
    def _(i):
        lhs = rows_of(block.at[0], jnp.where(i // 2 == 1, 1, 0))
        rhs = rows_of(block.at[i % 2], jnp.where(i < 2, 0, 1))
        found[i] = matmul(lhs, rhs)

    out[0] = found[0] + found[1]
    out[1] = found[2] + found[3]
    out[2], out[3] = found[4], found[5]


def stores(right, left, up, down, own):
    return {
        (0, 0): own.at[0],
        (0, 1): own.at[1],
        (1, 0): up,
        (1, 1): right.at[1],
        (2, 0): right.at[0],
        (2, 1): left.at[0],
        (3, 0): left.at[1],
        (3, 1): down,
    }


ORDER = ((2, 0), (1, 1), (2, 1), (3, 0), (1, 0), (3, 1), (0, 0), (0, 1))


def stack(refs, lefts, rights):
    side_by_side(lefts.at[0], refs[0], refs[1])
    side_by_side(lefts.at[1], refs[4], refs[5])
    side_by_side(rights.at[0], refs[2], refs[3])
    turned(rights.at[1], refs[2], refs[3])


def early_kernel(device, table, *refs):
    outs, lefts, rights = refs[6:16], refs[16], refs[17]
    stack(refs, lefts, rights)
    for t, j in ORDER:
        for color in range(2):
            index = table[device[0] * 16 + color * 8 + t * 2 + j]
            lhs = rows_of(lefts.at[index // 4], index // 2 % 2)
            rhs = rows_of(rights.at[color], index % 2)
            stores(*outs[5 * color : 5 * color + 5])[t, j][...] = matmul(lhs, rhs)


def late_kernel(device, table, diagonal, *refs):
    outs, lefts, rights = refs[6:16], refs[16], refs[17]
    stack(refs, lefts, rights)
    upper = (device[1] >= PLANES // 2).astype(jnp.int32)
    for t, j in ORDER:
        for color in range(2):
            index = table[device[0] * 16 + color * 8 + t * 2 + j]
            near = index < 4
            h = jnp.where(near, index // 2, index % 2)
            k = jnp.where(near, index % 2, (h + upper) % 2)
            lhs = rows_of(lefts.at[index // 4], h)
            product = matmul(lhs, rows_of(rights.at[color], k))
            ready = diagonal[jnp.maximum(index - 6, 0) * 2 + color]
            out = stores(*outs[5 * color : 5 * color + 5])[t, j]
            out[...] = jnp.where(index < 6, product, ready)


def finish_kernel(device, ahead, *refs):
    ins, outs, sums = refs[:20], refs[20:28], refs[28]
    slab = sums.shape[1] // 4
    for color in range(2):

        @pl.loop(0, 4)
        def _(i):
            rows = pl.ds(pl.multiple_of(i * slab, slab), slab)
            for group in range(2):
                own, right, left, right2, left2 = ins[10 * color + 5 * group :][:5]
                sums[2 * group, rows] = own[0, rows] + right2[rows] + left[1, rows]
                sums[2 * group + 1, rows] = own[1, rows] + right[1, rows] + left2[rows]

        @pl.loop(0, 4)
        def _(i):
            rows = pl.ds(pl.multiple_of(i * slab, slab), slab)
            for t in range(SIDE):
                outs[4 * color + t][rows] = sums[ahead[device[0] * 8 + color * 4 + t], rows]


def mirror_kernel(device, flags, *refs):
    p, q = [(refs[i][...] + refs[i + 2][...]) + (refs[i + 1][...] + refs[i + 3][...]) for i in (0, 4)]
    first, second = refs[8:]
    pt, qt = p.T, q.T
    flip = flags[device[0] * 2] == 1
    diagonal = flags[device[0] * 2 + 1] == 1
    first[0] = jnp.where(diagonal, 0.5 * (p + pt), jnp.where(flip, pt, p))
    first[1] = jnp.where(diagonal, 0.5 * (p - pt), jnp.where(flip, -qt, q))
    second[0] = jnp.where(diagonal, 0.5 * (q + qt), jnp.where(flip, p, pt))
    second[1] = jnp.where(diagonal, 0.5 * (q - qt), jnp.where(flip, q, -qt))


def kernel_call(kernel, scalars, blocks, shapes, flops=0, scratch=()):
    shapes = [jax.ShapeDtypeStruct(shape, jnp.float32) for shape in shapes]
    vmem = pl.BlockSpec(memory_space=pltpu.VMEM)
    smem = pl.BlockSpec(memory_space=pltpu.SMEM)
    moved = sum(v.size * v.dtype.itemsize for v in blocks) + sum(4 * v.size for v in shapes)
    return pl.pallas_call(
        kernel,
        out_shape=shapes,
        in_specs=[smem] * len(scalars) + [vmem] * len(blocks),
        out_specs=[vmem] * len(shapes),
        scratch_shapes=scratch,
        cost_estimate=pl.CostEstimate(flops=flops, bytes_accessed=moved, transcendentals=0),
    )(*scalars, *blocks)


def shift_x(value, step):
    pairs = [
        (y * SIDE + x, y * SIDE + (x + step) % SIDE) for y in range(SIDE) for x in range(SIDE)
    ]
    return lax.ppermute(value, "row", pairs)


def shift_y(value, step):
    pairs = [
        (y * SIDE + x, (y + step) % SIDE * SIDE + x) for y in range(SIDE) for x in range(SIDE)
    ]
    return lax.ppermute(value, "row", pairs)


def shift_z(value, step):
    return lax.ppermute(value, "col", [(c, (c + step) % PLANES) for c in range(PLANES)])


def ring_start(outs, shift):
    right, left, up, down, own = outs
    right, left = shift(right, 1), shift(left, -1)
    return own, right, left, up + right[0], down + left[0]


def ring_end(parts, shift):
    own, right, left, up, down = parts
    return own, right, left, shift(up, 1), shift(down, -1)


def direct(outs, shift):
    return (outs[0],) + tuple(shift(outs[t], t) for t in range(1, SIDE))


def exchange(parts, axis):
    count = lax.axis_size(axis)
    copies = jnp.broadcast_to(parts[None], (count,) + parts.shape)
    return lax.all_to_all(copies, axis, 0, 0)


def columns_to_rows(weight_real, weight_imag, power, gain):
    real = gain[0][None, :]
    imag = gain[1][None, :]
    return jnp.stack(
        [
            jnp.sum(weight_real * real + weight_imag * imag, axis=1),
            jnp.sum(weight_real * imag - weight_imag * real, axis=1),
            jnp.sum(power * (real * real + imag * imag), axis=1),
        ]
    )


def rows_to_columns(weight_real, weight_imag, power, gain):
    real = gain[0][:, None]
    imag = gain[1][:, None]
    return jnp.stack(
        [
            jnp.sum(weight_real * real - weight_imag * imag, axis=0),
            jnp.sum(weight_real * imag + weight_imag * real, axis=0),
            jnp.sum(power * (real * real + imag * imag), axis=0),
        ]
    )


def vis_tiles(samples, gain):
    row_index = lax.axis_index("row")
    column_index = lax.axis_index("col")
    first, second, early, late, ahead, flags, half = tables()
    device_index = row_index * PLANES + column_index
    device = jnp.stack([device_index, column_index]).astype(jnp.int32)
    here = samples[:, 0, :], samples[:, 1, :]
    antennas, times = here[0].shape
    quarter = antennas // 2
    product = 4 * quarter * quarter * times
    stacks = [pltpu.VMEM((2, antennas, 2 * times), here[0].dtype)] * 2
    found = stacks[0], pltpu.VMEM((6, quarter, quarter), jnp.float32)
    near = [(shift_z(part, -1), shift_z(part, 1)) for part in here]
    far = [(shift_z(above, -1), shift_z(below, 1)) for above, below in near]
    above, below = zip(*near)
    above2, below2 = zip(*far)
    gain, *free = lax.optimization_barrier((gain, *here))
    (diagonal,) = kernel_call(diagonal_kernel, (), free, [(4, quarter, quarter)], 6 * product, found)
    *below, diagonal = lax.optimization_barrier((*below, diagonal))
    shapes = 2 * ([(2, quarter, quarter)] * 2 + [(quarter, quarter)] * 2 + [(2, quarter, quarter)])
    outs = kernel_call(
        early_kernel,
        (device, jnp.asarray(early.reshape(-1))),
        (*here, *above, *below),
        shapes,
        16 * product,
        stacks,
    )
    along_x, along_y = ring_start(outs[:5], shift_x), ring_start(outs[5:], shift_y)
    sums = along_x[3:] + along_y[3:]
    *above2, first_below2, second_below2 = lax.optimization_barrier((*sums, *above2, *below2))[4:]
    early_parts = ring_end(along_x, shift_x), ring_end(along_y, shift_y)
    outs = kernel_call(
        late_kernel,
        (device, jnp.asarray(late.reshape(-1))),
        (diagonal, *below, *above2, first_below2, second_below2),
        shapes,
        12 * product,
        stacks,
    )
    late_parts = [
        ring_end(ring_start(part, shift), shift)
        for part, shift in ((outs[:5], shift_x), (outs[5:], shift_y))
    ]
    outs = kernel_call(
        finish_kernel,
        (device, jnp.asarray(ahead.reshape(-1))),
        early_parts[0] + late_parts[0] + early_parts[1] + late_parts[1],
        [(quarter, quarter)] * 8,
        scratch=(pltpu.VMEM((4, quarter, quarter), jnp.float32),),
    )
    parts = direct(outs[:4], shift_y) + direct(outs[4:], shift_x)
    one, two = kernel_call(
        mirror_kernel,
        (device, jnp.asarray(flags.reshape(-1))),
        parts,
        [(2, quarter, quarter)] * 2,
    )
    one = lax.ppermute(one, ("row", "col"), first)
    two = lax.ppermute(two, ("row", "col"), second)
    one_is_right = jnp.asarray(half)[device_index] == 1
    left = jnp.where(one_is_right, two, one)
    right = jnp.where(one_is_right, one, two)
    real = jnp.concatenate([left[0], right[0]], axis=1)
    imag = jnp.concatenate([left[1], right[1]], axis=1)
    return real, imag, gain


def starting_gains(initial_gains):
    blocks = SIDE * SIDE // PLANES
    pairs = [
        (r * PLANES + c, (r % blocks * PLANES + c) * PLANES + r // blocks)
        for r in range(SIDE * SIDE)
        for c in range(PLANES)
    ]
    share = lax.ppermute(initial_gains, ("row", "col"), pairs)
    return exchange(share, "row").transpose(1, 0, 2).reshape(2, -1)


def body(samples, sky_model, initial_gains):
    row_count = lax.axis_size("row")
    column_count = lax.axis_size("col")
    row_index = lax.axis_index("row")
    column_index = lax.axis_index("col")
    block_column = samples.shape[0]
    block_row = sky_model.shape[0]
    share_size = initial_gains.shape[1]
    blocks = block_column // block_row
    gain = starting_gains(initial_gains)
    vis_real, vis_imag, gain = vis_tiles(samples, gain)
    model_real = sky_model[:, 0, :].astype(jnp.float32)
    model_imag = sky_model[:, 1, :].astype(jnp.float32)
    global_rows = row_index * block_row + lax.broadcasted_iota(
        jnp.int32, (block_row, block_column), 0
    )
    global_columns = column_index * block_column + lax.broadcasted_iota(
        jnp.int32, (block_row, block_column), 1
    )
    cross_mask = (global_rows != global_columns).astype(jnp.float32)
    weight_real = (vis_real * model_real + vis_imag * model_imag) * cross_mask
    weight_imag = (vis_real * model_imag - vis_imag * model_real) * cross_mask
    power = (model_real * model_real + model_imag * model_imag) * cross_mask

    parts = columns_to_rows(weight_real, weight_imag, power, gain)
    sums = jnp.sum(exchange(parts, "col"), axis=0)
    gain = sums[:2] / sums[2:]

    parts = rows_to_columns(weight_real, weight_imag, power, gain)
    message = jnp.concatenate([parts.reshape(-1), gain.reshape(-1)])
    message = message.reshape(-1, 128)
    received = exchange(message, "row").reshape(row_count, -1)
    sums = jnp.sum(received[:, : 3 * block_column], axis=0).reshape(3, block_column)
    previous = lax.dynamic_slice_in_dim(
        received[:, 3 * block_column :], column_index * blocks, blocks, 0
    )
    previous = previous.reshape(blocks, 2, block_row).transpose(1, 0, 2).reshape(2, block_column)
    gain = 0.5 * (sums[:2] / sums[2:] + previous)

    parts = columns_to_rows(weight_real, weight_imag, power, gain)
    shares = parts.reshape(3, column_count, share_size).transpose(1, 0, 2)
    sums = jnp.sum(lax.all_to_all(shares, "col", 0, 0), axis=0)
    return sums[:2] / sums[2:]


def solution(mesh):
    return jax.shard_map(
        body,
        mesh=mesh,
        in_specs=(
            P(("chan", "col"), None, "row"),
            P(("chan", "row"), None, "col"),
            P(None, ("chan", "row", "col")),
        ),
        out_specs=P(None, ("chan", "row", "col")),
        check_vma=False,
    )
```

```python
import functools

import functools

import jax
import jax.numpy as jnp
import numpy as np
from jax import lax
from jax.experimental import pallas as pl
from jax.experimental.pallas import tpu as pltpu
from jax.sharding import PartitionSpec as P


SIDE = 4
PLANES = 8

OFFSETS = {0: (0, 0), 1: (0, 1), 2: (-1, 1), 3: (-1, 2), 4: (-2, 2)}
EARLY = [(d, h, k) for d in (1, 2) for h in (0, 1) for k in (0, 1)]
LATE = [(3, h, k) for h in (0, 1) for k in (0, 1)] + [(4, 0, 0), (4, 1, 1), (0, 0, 0), (0, 0, 1)]
PLACE = [
    [7, 0, 2, 5, 13, 10, 8, 15, 14, 6, 3, 12, 11, 9, 1, 4],
    [15, 10, 8, 2, 0, 7, 5, 13, 9, 4, 1, 14, 6, 11, 12, 3],
    [13, 8, 5, 10, 2, 0, 7, 15, 11, 14, 3, 1, 12, 9, 6, 4],
    [10, 13, 15, 2, 0, 8, 7, 5, 11, 4, 14, 9, 1, 12, 3, 6],
    [15, 8, 13, 10, 2, 5, 7, 0, 11, 6, 4, 14, 3, 1, 12, 9],
    [2, 10, 15, 0, 8, 5, 7, 13, 11, 12, 14, 9, 3, 1, 6, 4],
    [15, 0, 2, 13, 5, 8, 10, 7, 9, 14, 3, 11, 6, 4, 1, 12],
    [2, 5, 7, 10, 8, 0, 15, 13, 3, 12, 9, 1, 4, 6, 11, 14],
]


def targets(chunk, c):
    d, h, k = chunk
    a, b = [(c + offset) % PLANES for offset in OFFSETS[d]]
    if d == 0 and k == 0:
        return (2 * c, c, 0), (2 * c + 1, c, 1), 0
    if d == 0:
        return (2 * c + 1, c, 0), (2 * c, c, 1), 1
    if d == 4:
        k = h if c < PLANES // 2 else 1 - h
    plain, mirror = (2 * a + h, b, k), (2 * b + k, a, h)
    if d == 4 or h == k:
        return plain, mirror, 0
    return mirror, plain, 1


def tables():
    rows = SIDE * SIDE
    devices = rows * PLANES
    first, second = [], []
    early = np.zeros((devices, 2, SIDE, 2), np.int32)
    late = np.zeros((devices, 2, SIDE, 2), np.int32)
    ahead = np.zeros((devices, 2, SIDE), np.int32)
    flags = np.zeros((devices, 2), np.int32)
    half = np.zeros(devices, np.int32)
    for c in range(PLANES):
        for chunk, r in zip(EARLY + LATE, PLACE[c]):
            one, two, conjugated = targets(chunk, c)
            first.append((r * PLANES + c, one[0] * PLANES + one[1]))
            second.append((r * PLANES + c, two[0] * PLANES + two[1]))
            flags[r * PLANES + c] = conjugated, chunk == (0, 0, 0)
            half[one[0] * PLANES + one[1]] = one[2]
        for i, owner in enumerate(PLACE[c]):
            v, u = owner // SIDE, owner % SIDE
            order, index = (early, i) if i < len(EARLY) else (late, i - len(EARLY))
            for r in range(rows):
                y, x = r // SIDE, r % SIDE
                order[r * PLANES + c, 0, (u - x) % SIDE, v // 2] = index
                order[r * PLANES + c, 1, (v - y) % SIDE, u // 2] = index
        for r in range(rows):
            y, x = r // SIDE, r % SIDE
            for t in range(SIDE):
                v, u = (y + t) % SIDE, (x + t) % SIDE
                ahead[r * PLANES + c, 0, t] = (v + x) % 2 * 2 + v // 2
                ahead[r * PLANES + c, 1, t] = (u + y) % 2 * 2 + u // 2
    return first, second, early, late, ahead, flags, half


def matmul(lhs, rhs):
    return lax.dot_general(lhs, rhs, (((1,), (1,)), ((), ())), preferred_element_type=jnp.float32)


def rows_of(ref, half):
    quarter = ref.shape[0] // 2
    return ref[pl.ds(pl.multiple_of(half * quarter, quarter), quarter), :]


def side_by_side(out, real, imag, turned=False):
    antennas, times = real.shape
    slab = antennas // 4

    @pl.loop(0, 4)
    def _(i):
        rows = pl.ds(pl.multiple_of(i * slab, slab), slab)
        out[rows, :times] = -imag[rows, :] if turned else real[rows, :]
        out[rows, times:] = real[rows, :] if turned else imag[rows, :]


def diagonal_kernel(real, imag, out, block, found):
    side_by_side(block.at[0], real, imag)
    side_by_side(block.at[1], real, imag, turned=True)

    @pl.loop(0, 6)
    def _(i):
        lhs = rows_of(block.at[0], jnp.where(i // 2 == 1, 1, 0))
        rhs = rows_of(block.at[i % 2], jnp.where(i < 2, 0, 1))
        found[i] = matmul(lhs, rhs)

    out[0] = found[0] + found[1]
    out[1] = found[2] + found[3]
    out[2], out[3] = found[4], found[5]


FIRST = (((2, 0), (1, 1)), ((2, 1), (3, 0)))
REST = (((1, 0), (3, 1)), ((0, 0), (0, 1)))


def stack(refs, lefts, rights):
    side_by_side(lefts.at[0], refs[0], refs[1])
    side_by_side(lefts.at[1], refs[4], refs[5])
    side_by_side(rights.at[0], refs[2], refs[3])
    side_by_side(rights.at[1], refs[2], refs[3], turned=True)


def early_kernel(entries, device, table, *refs):
    outs, lefts, rights = refs[6:10], refs[10], refs[11]
    stack(refs, lefts, rights)
    for out in range(2):
        for place, (t, j) in enumerate(entries[out]):
            for color in range(2):
                index = table[device[0] * 16 + color * 8 + t * 2 + j]
                lhs = rows_of(lefts.at[index // 4], index // 2 % 2)
                rhs = rows_of(rights.at[color], index % 2)
                outs[2 * color + out][place] = matmul(lhs, rhs)


def late_kernel(entries, device, table, *refs):
    diagonal, outs, lefts, rights = refs[6], refs[7:11], refs[11], refs[12]
    stack(refs, lefts, rights)
    upper = (device[1] >= PLANES // 2).astype(jnp.int32)
    for out in range(2):
        for place, (t, j) in enumerate(entries[out]):
            for color in range(2):
                index = table[device[0] * 16 + color * 8 + t * 2 + j]
                near = index < 4
                h = jnp.where(near, index // 2, index % 2)
                k = jnp.where(near, index % 2, (h + upper) % 2)
                lhs = rows_of(lefts.at[index // 4], h)
                product = matmul(lhs, rows_of(rights.at[color], k))
                ready = diagonal[jnp.maximum(index - 6, 0) * 2 + color]
                outs[2 * color + out][place] = jnp.where(index < 6, product, ready)


def finish_kernel(device, ahead, *refs):
    ins, outs, sums = refs[:20], refs[20:28], refs[28]
    for color in range(2):
        for group in range(2):
            own, right, left, right2, left2 = ins[10 * color + 5 * group :][:5]
            sums[2 * group] = own[0] + right2[...] + left[0]
            sums[2 * group + 1] = own[1] + right[0] + left2[...]
        for t in range(SIDE):
            outs[4 * color + t][...] = sums[ahead[device[0] * 8 + color * 4 + t]]


def finish(device, ahead, parts):
    slabs = 4
    quarter = parts[0].shape[-1]
    slab = quarter // slabs
    smem = pl.BlockSpec(memory_space=pltpu.SMEM)
    one = pl.BlockSpec((slab, quarter), lambda i: (i, 0))
    second = pl.BlockSpec((1, slab, quarter), lambda i: (1, i, 0))
    both = pl.BlockSpec((2, slab, quarter), lambda i: (0, i, 0))
    return pl.pallas_call(
        finish_kernel,
        grid=(slabs,),
        out_shape=[jax.ShapeDtypeStruct((quarter, quarter), jnp.float32)] * 8,
        in_specs=[smem, smem] + 4 * [both, second, second, one, one],
        out_specs=[one] * 8,
        scratch_shapes=[pltpu.VMEM((4, slab, quarter), jnp.float32)],
        cost_estimate=pl.CostEstimate(
            flops=16 * quarter * quarter, bytes_accessed=128 * quarter * quarter, transcendentals=0
        ),
    )(device, ahead, *parts)


def mirror_kernel(device, flags, *refs):
    p, q = [(refs[i][...] + refs[i + 2][...]) + (refs[i + 1][...] + refs[i + 3][...]) for i in (0, 4)]
    first, second = refs[8:]
    pt, qt = p.T, q.T
    flip = flags[device[0] * 2] == 1
    diagonal = flags[device[0] * 2 + 1] == 1
    first[0] = jnp.where(diagonal, 0.5 * (p + pt), jnp.where(flip, pt, p))
    first[1] = jnp.where(diagonal, 0.5 * (p - pt), jnp.where(flip, -qt, q))
    second[0] = jnp.where(diagonal, 0.5 * (q + qt), jnp.where(flip, p, pt))
    second[1] = jnp.where(diagonal, 0.5 * (q - qt), jnp.where(flip, q, -qt))


def kernel_call(kernel, scalars, blocks, shapes, flops=0, scratch=()):
    shapes = [jax.ShapeDtypeStruct(shape, jnp.float32) for shape in shapes]
    vmem = pl.BlockSpec(memory_space=pltpu.VMEM)
    smem = pl.BlockSpec(memory_space=pltpu.SMEM)
    moved = sum(v.size * v.dtype.itemsize for v in blocks) + sum(4 * v.size for v in shapes)
    return pl.pallas_call(
        kernel,
        out_shape=shapes,
        in_specs=[smem] * len(scalars) + [vmem] * len(blocks),
        out_specs=[vmem] * len(shapes),
        scratch_shapes=scratch,
        cost_estimate=pl.CostEstimate(flops=flops, bytes_accessed=moved, transcendentals=0),
    )(*scalars, *blocks)


def shift_x(value, step):
    pairs = [
        (y * SIDE + x, y * SIDE + (x + step) % SIDE) for y in range(SIDE) for x in range(SIDE)
    ]
    return lax.ppermute(value, "row", pairs)


def shift_y(value, step):
    pairs = [
        (y * SIDE + x, (y + step) % SIDE * SIDE + x) for y in range(SIDE) for x in range(SIDE)
    ]
    return lax.ppermute(value, "row", pairs)


def shift_z(value, step):
    return lax.ppermute(value, "col", [(c, (c + step) % PLANES) for c in range(PLANES)])


def ring_start(right, left, shift):
    return shift(right, 1), shift(left, -1)


def ring_sums(received, rest):
    right, left = received
    return rest[0] + right[0], rest[1] + left[0]


def ring_end(own, received, sums, shift):
    return own, *received, shift(sums[0], 1), shift(sums[1], -1)


def direct(outs, shift):
    return (outs[0],) + tuple(shift(outs[t], t) for t in range(1, SIDE))


def exchange(parts, axis):
    count = lax.axis_size(axis)
    copies = jnp.broadcast_to(parts[None], (count,) + parts.shape)
    return lax.all_to_all(copies, axis, 0, 0)


def columns_to_rows(weight_real, weight_imag, power, gain):
    real = gain[0][None, :]
    imag = gain[1][None, :]
    return jnp.stack(
        [
            jnp.sum(weight_real * real + weight_imag * imag, axis=1),
            jnp.sum(weight_real * imag - weight_imag * real, axis=1),
            jnp.sum(power * (real * real + imag * imag), axis=1),
        ]
    )


def rows_to_columns(weight_real, weight_imag, power, gain):
    real = gain[0][:, None]
    imag = gain[1][:, None]
    return jnp.stack(
        [
            jnp.sum(weight_real * real - weight_imag * imag, axis=0),
            jnp.sum(weight_real * imag + weight_imag * real, axis=0),
            jnp.sum(power * (real * real + imag * imag), axis=0),
        ]
    )


def vis_tiles(samples, gain):
    row_index = lax.axis_index("row")
    column_index = lax.axis_index("col")
    first, second, early, late, ahead, flags, half = tables()
    device_index = row_index * PLANES + column_index
    device = jnp.stack([device_index, column_index]).astype(jnp.int32)
    real, later = lax.optimization_barrier((samples[:, 0, :], samples))
    here = real, later[:, 1, :]
    antennas, times = real.shape
    quarter = antennas // 2
    product = 4 * quarter * quarter * times
    stacks = [pltpu.VMEM((2, antennas, 2 * times), real.dtype)] * 2
    found = stacks[0], pltpu.VMEM((6, quarter, quarter), jnp.float32)
    near = [(shift_z(part, -1), shift_z(part, 1)) for part in here]
    gain, near[0] = lax.optimization_barrier((gain, near[0]))
    far = [(shift_z(above, -1), shift_z(below, 1)) for above, below in near]
    above, below = zip(*near)
    above2, below2 = zip(*far)
    shapes = [(2, quarter, quarter)] * 4
    axes = (shift_x, shift_y)

    def chunks(kernel, entries, table, blocks, products):
        return kernel_call(
            functools.partial(kernel, entries),
            (device, jnp.asarray(table.reshape(-1))),
            blocks,
            shapes,
            products * product,
            stacks,
        )

    blocks = *here, *above, *below
    first_outs = chunks(early_kernel, FIRST, early, blocks, 8)
    received = [ring_start(*first_outs[2 * i : 2 * i + 2], axes[i]) for i in range(2)]
    outs = chunks(early_kernel, REST, early, blocks, 8)
    (diagonal,) = kernel_call(diagonal_kernel, (), here, [(4, quarter, quarter)], 6 * product, found)
    sums = [ring_sums(received[i], outs[2 * i]) for i in range(2)]
    early_parts = [ring_end(outs[2 * i + 1], received[i], sums[i], axes[i]) for i in range(2)]
    _, blocks = lax.optimization_barrier((sums, (*below, *above2, *below2, diagonal)))
    first_outs = chunks(late_kernel, FIRST, late, blocks, 8)
    received = [ring_start(*first_outs[2 * i : 2 * i + 2], axes[i]) for i in range(2)]
    outs = chunks(late_kernel, REST, late, blocks, 8)
    sums = [ring_sums(received[i], outs[2 * i]) for i in range(2)]
    late_parts = [ring_end(outs[2 * i + 1], received[i], sums[i], axes[i]) for i in range(2)]
    outs = finish(
        device,
        jnp.asarray(ahead.reshape(-1)),
        early_parts[0] + late_parts[0] + early_parts[1] + late_parts[1],
    )
    parts = direct(outs[:4], shift_y) + direct(outs[4:], shift_x)
    one, two = kernel_call(
        mirror_kernel,
        (device, jnp.asarray(flags.reshape(-1))),
        parts,
        [(2, quarter, quarter)] * 2,
    )
    one = lax.ppermute(one, ("row", "col"), first)
    two = lax.ppermute(two, ("row", "col"), second)
    one_is_right = jnp.asarray(half)[device_index] == 1
    left = jnp.where(one_is_right, two, one)
    right = jnp.where(one_is_right, one, two)
    real = jnp.concatenate([left[0], right[0]], axis=1)
    imag = jnp.concatenate([left[1], right[1]], axis=1)
    return real, imag, gain


def starting_gains(initial_gains):
    blocks = SIDE * SIDE // PLANES
    pairs = [
        (r * PLANES + c, (r % blocks * PLANES + c) * PLANES + r // blocks)
        for r in range(SIDE * SIDE)
        for c in range(PLANES)
    ]
    share = lax.ppermute(initial_gains, ("row", "col"), pairs)
    return exchange(share, "row").transpose(1, 0, 2).reshape(2, -1)


def body(samples, sky_model, initial_gains):
    row_count = lax.axis_size("row")
    column_count = lax.axis_size("col")
    row_index = lax.axis_index("row")
    column_index = lax.axis_index("col")
    block_column = samples.shape[0]
    block_row = sky_model.shape[0]
    share_size = initial_gains.shape[1]
    blocks = block_column // block_row
    gain = starting_gains(initial_gains)
    vis_real, vis_imag, gain = vis_tiles(samples, gain)
    model_real = sky_model[:, 0, :].astype(jnp.float32)
    model_imag = sky_model[:, 1, :].astype(jnp.float32)
    global_rows = row_index * block_row + lax.broadcasted_iota(
        jnp.int32, (block_row, block_column), 0
    )
    global_columns = column_index * block_column + lax.broadcasted_iota(
        jnp.int32, (block_row, block_column), 1
    )
    cross_mask = (global_rows != global_columns).astype(jnp.float32)
    weight_real = (vis_real * model_real + vis_imag * model_imag) * cross_mask
    weight_imag = (vis_real * model_imag - vis_imag * model_real) * cross_mask
    power = (model_real * model_real + model_imag * model_imag) * cross_mask

    parts = columns_to_rows(weight_real, weight_imag, power, gain)
    sums = jnp.sum(exchange(parts, "col"), axis=0)
    gain = sums[:2] / sums[2:]

    parts = rows_to_columns(weight_real, weight_imag, power, gain)
    message = jnp.concatenate([parts.reshape(-1), gain.reshape(-1)])
    message = message.reshape(-1, 128)
    received = exchange(message, "row").reshape(row_count, -1)
    sums = jnp.sum(received[:, : 3 * block_column], axis=0).reshape(3, block_column)
    previous = lax.dynamic_slice_in_dim(
        received[:, 3 * block_column :], column_index * blocks, blocks, 0
    )
    previous = previous.reshape(blocks, 2, block_row).transpose(1, 0, 2).reshape(2, block_column)
    gain = 0.5 * (sums[:2] / sums[2:] + previous)

    parts = columns_to_rows(weight_real, weight_imag, power, gain)
    shares = parts.reshape(3, column_count, share_size).transpose(1, 0, 2)
    sums = jnp.sum(lax.all_to_all(shares, "col", 0, 0), axis=0)
    return sums[:2] / sums[2:]


def solution(mesh):
    return jax.shard_map(
        body,
        mesh=mesh,
        in_specs=(
            P(("chan", "col"), None, "row"),
            P(("chan", "row"), None, "col"),
            P(None, ("chan", "row", "col")),
        ),
        out_specs=P(None, ("chan", "row", "col")),
        check_vma=False,
    )
```

```python
import jax
import jax.numpy as jnp
import numpy as np
from jax import lax
from jax.experimental import pallas as pl
from jax.experimental.pallas import tpu as pltpu
from jax.sharding import PartitionSpec as P


SIDE = 4
PLANES = 8

OFFSETS = {0: (0, 0), 1: (0, 1), 2: (-1, 1), 3: (-1, 2), 4: (-2, 2)}
EARLY = [(d, h, k) for d in (1, 2) for h in (0, 1) for k in (0, 1)]
LATE = [(3, h, k) for h in (0, 1) for k in (0, 1)] + [(4, 0, 0), (4, 1, 1), (0, 0, 0), (0, 0, 1)]
PLACE = [
    [7, 0, 2, 5, 13, 10, 8, 15, 14, 6, 3, 12, 11, 9, 1, 4],
    [15, 10, 8, 2, 0, 7, 5, 13, 9, 4, 1, 14, 6, 11, 12, 3],
    [13, 8, 5, 10, 2, 0, 7, 15, 11, 14, 3, 1, 12, 9, 6, 4],
    [10, 13, 15, 2, 0, 8, 7, 5, 11, 4, 14, 9, 1, 12, 3, 6],
    [15, 8, 13, 10, 2, 5, 7, 0, 11, 6, 4, 14, 3, 1, 12, 9],
    [2, 10, 15, 0, 8, 5, 7, 13, 11, 12, 14, 9, 3, 1, 6, 4],
    [15, 0, 2, 13, 5, 8, 10, 7, 9, 14, 3, 11, 6, 4, 1, 12],
    [2, 5, 7, 10, 8, 0, 15, 13, 3, 12, 9, 1, 4, 6, 11, 14],
]


def targets(chunk, c):
    d, h, k = chunk
    a, b = [(c + offset) % PLANES for offset in OFFSETS[d]]
    if d == 0 and k == 0:
        return (2 * c, c, 0), (2 * c + 1, c, 1), 0
    if d == 0:
        return (2 * c + 1, c, 0), (2 * c, c, 1), 1
    if d == 4:
        k = h if c < PLANES // 2 else 1 - h
    plain, mirror = (2 * a + h, b, k), (2 * b + k, a, h)
    if d == 4 or h == k:
        return plain, mirror, 0
    return mirror, plain, 1


def tables():
    rows = SIDE * SIDE
    devices = rows * PLANES
    first, second = [], []
    early = np.zeros((devices, 2, SIDE, 2), np.int32)
    late = np.zeros((devices, 2, SIDE, 2), np.int32)
    ahead = np.zeros((devices, 2, SIDE), np.int32)
    flags = np.zeros((devices, 2), np.int32)
    half = np.zeros(devices, np.int32)
    for c in range(PLANES):
        for chunk, r in zip(EARLY + LATE, PLACE[c]):
            one, two, conjugated = targets(chunk, c)
            first.append((r * PLANES + c, one[0] * PLANES + one[1]))
            second.append((r * PLANES + c, two[0] * PLANES + two[1]))
            flags[r * PLANES + c] = conjugated, chunk == (0, 0, 0)
            half[one[0] * PLANES + one[1]] = one[2]
        for i, owner in enumerate(PLACE[c]):
            v, u = owner // SIDE, owner % SIDE
            order, index = (early, i) if i < len(EARLY) else (late, i - len(EARLY))
            for r in range(rows):
                y, x = r // SIDE, r % SIDE
                order[r * PLANES + c, 0, (u - x) % SIDE, v // 2] = index
                order[r * PLANES + c, 1, (v - y) % SIDE, u // 2] = index
        for r in range(rows):
            y, x = r // SIDE, r % SIDE
            for t in range(SIDE):
                v, u = (y + t) % SIDE, (x + t) % SIDE
                ahead[r * PLANES + c, 0, t] = (v + x) % 2 * 2 + v // 2
                ahead[r * PLANES + c, 1, t] = (u + y) % 2 * 2 + u // 2
    return first, second, early, late, ahead, flags, half


def matmul(lhs, rhs):
    return lax.dot_general(lhs, rhs, (((1,), (1,)), ((), ())), preferred_element_type=jnp.float32)


def rows_of(ref, half):
    quarter = ref.shape[0] // 2
    return ref[pl.ds(pl.multiple_of(half * quarter, quarter), quarter), :]


def slabs(rows, count=4):
    def run(function):
        @pl.loop(0, count)
        def _(i):
            function(pl.ds(pl.multiple_of(i * (rows // count), rows // count), rows // count))

    return run


def turn(out, block):
    times = block.shape[1] // 2

    @slabs(block.shape[0])
    def _(rows):
        out[rows, :times] = -block[rows, times:]
        out[rows, times:] = block[rows, :times]


def diagonal_kernel(block, out, turned, found):
    turn(turned, block)
    for part, rhs in enumerate((block, turned)):

        @pl.loop(0, 3)
        def _(i):
            lhs = rows_of(block, jnp.where(i == 1, 1, 0))
            found[2 * i + part] = matmul(lhs, rows_of(rhs, jnp.where(i == 0, 0, 1)))

    out[0] = found[0] + found[1]
    out[1] = found[2] + found[3]
    out[2], out[3] = found[4], found[5]


ORDER = ((2, 0), (1, 1), (2, 1), (3, 0), (1, 0), (3, 1), (0, 0), (0, 1))


def stores(right, left, up, down, own):
    return {
        (0, 0): own.at[0],
        (0, 1): own.at[1],
        (1, 0): up,
        (1, 1): right.at[1],
        (2, 0): right.at[0],
        (2, 1): left.at[0],
        (3, 0): left.at[1],
        (3, 1): down,
    }


def stack(lefts, one, two):
    @slabs(one.shape[0])
    def _(rows):
        lefts[0, rows], lefts[1, rows] = one[rows], two[rows]


def early_kernel(device, table, one, two, block, *refs):
    outs, lefts, turned = refs[:10], refs[10], refs[11]
    stack(lefts, one, two)
    turn(turned, block)
    for t, j in ORDER:
        for color, rhs in enumerate((block, turned)):
            index = table[device[0] * 16 + color * 8 + t * 2 + j]
            lhs = rows_of(lefts.at[index // 4], index // 2 % 2)
            out = stores(*outs[5 * color : 5 * color + 5])[t, j]
            out[...] = matmul(lhs, rows_of(rhs, index % 2))


def late_kernel(device, table, one, two, block, diagonal, *refs):
    outs, lefts, turned = refs[:10], refs[10], refs[11]
    stack(lefts, one, two)
    turn(turned, block)
    upper = (device[1] >= PLANES // 2).astype(jnp.int32)
    for t, j in ORDER:
        for color, rhs in enumerate((block, turned)):
            index = table[device[0] * 16 + color * 8 + t * 2 + j]
            near = index < 4
            h = jnp.where(near, index // 2, index % 2)
            k = jnp.where(near, index % 2, (h + upper) % 2)
            product = matmul(rows_of(lefts.at[index // 4], h), rows_of(rhs, k))
            ready = diagonal[jnp.maximum(index - 6, 0) * 2 + color]
            out = stores(*outs[5 * color : 5 * color + 5])[t, j]
            out[...] = jnp.where(index < 6, product, ready)


def finish_kernel(device, ahead, *refs):
    ins, outs, sums = refs[:20], refs[20:28], refs[28]
    for color in range(2):
        for group in range(2):
            own, right, left, right2, left2 = ins[10 * color + 5 * group :][:5]
            sums[2 * group] = own[0] + right2[...] + left[0]
            sums[2 * group + 1] = own[1] + right[0] + left2[...]
        for t in range(SIDE):
            outs[4 * color + t][...] = sums[ahead[device[0] * 8 + color * 4 + t]]


def finish(device, ahead, parts):
    steps = 4
    quarter = parts[0].shape[-1]
    slab = quarter // steps
    smem = pl.BlockSpec(memory_space=pltpu.SMEM)
    one = pl.BlockSpec((slab, quarter), lambda i: (i, 0))
    second = pl.BlockSpec((1, slab, quarter), lambda i: (1, i, 0))
    both = pl.BlockSpec((2, slab, quarter), lambda i: (0, i, 0))
    return pl.pallas_call(
        finish_kernel,
        grid=(steps,),
        out_shape=[jax.ShapeDtypeStruct((quarter, quarter), jnp.float32)] * 8,
        in_specs=[smem, smem] + 4 * [both, second, second, one, one],
        out_specs=[one] * 8,
        scratch_shapes=[pltpu.VMEM((4, slab, quarter), jnp.float32)],
        cost_estimate=pl.CostEstimate(
            flops=16 * quarter * quarter, bytes_accessed=128 * quarter * quarter, transcendentals=0
        ),
    )(device, ahead, *parts)


def mirror_kernel(device, flags, *refs):
    p, q = [(refs[i][...] + refs[i + 2][...]) + (refs[i + 1][...] + refs[i + 3][...]) for i in (0, 4)]
    first, second = refs[8:]
    pt, qt = p.T, q.T
    flip = flags[device[0] * 2] == 1
    diagonal = flags[device[0] * 2 + 1] == 1
    first[0] = jnp.where(diagonal, 0.5 * (p + pt), jnp.where(flip, pt, p))
    first[1] = jnp.where(diagonal, 0.5 * (p - pt), jnp.where(flip, -qt, q))
    second[0] = jnp.where(diagonal, 0.5 * (q + qt), jnp.where(flip, p, pt))
    second[1] = jnp.where(diagonal, 0.5 * (q - qt), jnp.where(flip, q, -qt))


def kernel_call(kernel, scalars, blocks, shapes, flops=0, scratch=()):
    shapes = [jax.ShapeDtypeStruct(shape, jnp.float32) for shape in shapes]
    vmem = pl.BlockSpec(memory_space=pltpu.VMEM)
    smem = pl.BlockSpec(memory_space=pltpu.SMEM)
    moved = sum(v.size * v.dtype.itemsize for v in blocks) + sum(4 * v.size for v in shapes)
    return pl.pallas_call(
        kernel,
        out_shape=shapes,
        in_specs=[smem] * len(scalars) + [vmem] * len(blocks),
        out_specs=[vmem] * len(shapes),
        scratch_shapes=scratch,
        cost_estimate=pl.CostEstimate(flops=flops, bytes_accessed=moved, transcendentals=0),
    )(*scalars, *blocks)


def shift_x(value, step):
    pairs = [
        (y * SIDE + x, y * SIDE + (x + step) % SIDE) for y in range(SIDE) for x in range(SIDE)
    ]
    return lax.ppermute(value, "row", pairs)


def shift_y(value, step):
    pairs = [
        (y * SIDE + x, (y + step) % SIDE * SIDE + x) for y in range(SIDE) for x in range(SIDE)
    ]
    return lax.ppermute(value, "row", pairs)


def shift_z(value, step):
    return lax.ppermute(value, "col", [(c, (c + step) % PLANES) for c in range(PLANES)])


def ring_start(right, left, shift):
    return shift(right, 1), shift(left, -1)


def ring_sums(received, rest):
    right, left = received
    return rest[0] + right[0], rest[1] + left[0]


def ring_end(own, received, sums, shift):
    return own, *received, shift(sums[0], 1), shift(sums[1], -1)


def direct(outs, shift):
    return (outs[0],) + tuple(shift(outs[t], t) for t in range(1, SIDE))


def exchange(parts, axis):
    count = lax.axis_size(axis)
    copies = jnp.broadcast_to(parts[None], (count,) + parts.shape)
    return lax.all_to_all(copies, axis, 0, 0)


def columns_to_rows(weight_real, weight_imag, power, gain):
    real = gain[0][None, :]
    imag = gain[1][None, :]
    return jnp.stack(
        [
            jnp.sum(weight_real * real + weight_imag * imag, axis=1),
            jnp.sum(weight_real * imag - weight_imag * real, axis=1),
            jnp.sum(power * (real * real + imag * imag), axis=1),
        ]
    )


def rows_to_columns(weight_real, weight_imag, power, gain):
    real = gain[0][:, None]
    imag = gain[1][:, None]
    return jnp.stack(
        [
            jnp.sum(weight_real * real - weight_imag * imag, axis=0),
            jnp.sum(weight_real * imag + weight_imag * real, axis=0),
            jnp.sum(power * (real * real + imag * imag), axis=0),
        ]
    )


def vis_tiles(samples, gain):
    row_index = lax.axis_index("row")
    column_index = lax.axis_index("col")
    first, second, early, late, ahead, flags, half = tables()
    device_index = row_index * PLANES + column_index
    device = jnp.stack([device_index, column_index]).astype(jnp.int32)
    here = samples.reshape(samples.shape[0], -1)
    antennas, times = here.shape
    quarter = antennas // 2
    product = 2 * quarter * quarter * times
    turned = pltpu.VMEM(here.shape, here.dtype)
    stacks = pltpu.VMEM((2,) + here.shape, here.dtype), turned
    found = turned, pltpu.VMEM((6, quarter, quarter), jnp.float32)
    above, below = shift_z(here, -1), shift_z(here, 1)
    gain, above, below = lax.optimization_barrier((gain, above, below))
    above2, below2 = shift_z(above, -1), shift_z(below, 1)
    shapes = 2 * ([(2, quarter, quarter)] * 2 + [(quarter, quarter)] * 2 + [(2, quarter, quarter)])
    axes = (shift_x, shift_y)

    def chunks(kernel, table, blocks):
        scalars = device, jnp.asarray(table.reshape(-1))
        return kernel_call(kernel, scalars, blocks, shapes, 16 * product, stacks)

    outs = chunks(early_kernel, early, (here, below, above))
    received = [ring_start(*outs[5 * i : 5 * i + 2], axes[i]) for i in range(2)]
    (diagonal,) = kernel_call(
        diagonal_kernel, (), (here,), [(4, quarter, quarter)], 6 * product, found
    )
    sums = [ring_sums(received[i], outs[5 * i + 2 : 5 * i + 4]) for i in range(2)]
    early_parts = [ring_end(outs[5 * i + 4], received[i], sums[i], axes[i]) for i in range(2)]
    _, blocks = lax.optimization_barrier((sums, (below, below2, above2, diagonal)))
    outs = chunks(late_kernel, late, blocks)
    received = [ring_start(*outs[5 * i : 5 * i + 2], axes[i]) for i in range(2)]
    sums = [ring_sums(received[i], outs[5 * i + 2 : 5 * i + 4]) for i in range(2)]
    late_parts = [ring_end(outs[5 * i + 4], received[i], sums[i], axes[i]) for i in range(2)]
    outs = finish(
        device,
        jnp.asarray(ahead.reshape(-1)),
        early_parts[0] + late_parts[0] + early_parts[1] + late_parts[1],
    )
    parts = direct(outs[:4], shift_y) + direct(outs[4:], shift_x)
    one, two = kernel_call(
        mirror_kernel,
        (device, jnp.asarray(flags.reshape(-1))),
        parts,
        [(2, quarter, quarter)] * 2,
    )
    one = lax.ppermute(one, ("row", "col"), first)
    two = lax.ppermute(two, ("row", "col"), second)
    one_is_right = jnp.asarray(half)[device_index] == 1
    left = jnp.where(one_is_right, two, one)
    right = jnp.where(one_is_right, one, two)
    real = jnp.concatenate([left[0], right[0]], axis=1)
    imag = jnp.concatenate([left[1], right[1]], axis=1)
    return real, imag, gain


def starting_gains(initial_gains):
    blocks = SIDE * SIDE // PLANES
    pairs = [
        (r * PLANES + c, (r % blocks * PLANES + c) * PLANES + r // blocks)
        for r in range(SIDE * SIDE)
        for c in range(PLANES)
    ]
    share = lax.ppermute(initial_gains, ("row", "col"), pairs)
    return exchange(share, "row").transpose(1, 0, 2).reshape(2, -1)


def body(samples, sky_model, initial_gains):
    row_count = lax.axis_size("row")
    column_count = lax.axis_size("col")
    row_index = lax.axis_index("row")
    column_index = lax.axis_index("col")
    block_column = samples.shape[0]
    block_row = sky_model.shape[0]
    share_size = initial_gains.shape[1]
    blocks = block_column // block_row
    gain = starting_gains(initial_gains)
    vis_real, vis_imag, gain = vis_tiles(samples, gain)
    model_real = sky_model[:, 0, :].astype(jnp.float32)
    model_imag = sky_model[:, 1, :].astype(jnp.float32)
    global_rows = row_index * block_row + lax.broadcasted_iota(
        jnp.int32, (block_row, block_column), 0
    )
    global_columns = column_index * block_column + lax.broadcasted_iota(
        jnp.int32, (block_row, block_column), 1
    )
    cross_mask = (global_rows != global_columns).astype(jnp.float32)
    weight_real = (vis_real * model_real + vis_imag * model_imag) * cross_mask
    weight_imag = (vis_real * model_imag - vis_imag * model_real) * cross_mask
    power = (model_real * model_real + model_imag * model_imag) * cross_mask

    parts = columns_to_rows(weight_real, weight_imag, power, gain)
    sums = jnp.sum(exchange(parts.reshape(-1, 128), "col"), axis=0).reshape(parts.shape)
    gain = sums[:2] / sums[2:]

    parts = rows_to_columns(weight_real, weight_imag, power, gain)
    message = jnp.concatenate([parts.reshape(-1), gain.reshape(-1)])
    message = message.reshape(-1, 128)
    received = exchange(message, "row").reshape(row_count, -1)
    sums = jnp.sum(received[:, : 3 * block_column], axis=0).reshape(3, block_column)
    previous = lax.dynamic_slice_in_dim(
        received[:, 3 * block_column :], column_index * blocks, blocks, 0
    )
    previous = previous.reshape(blocks, 2, block_row).transpose(1, 0, 2).reshape(2, block_column)
    gain = 0.5 * (sums[:2] / sums[2:] + previous)

    parts = columns_to_rows(weight_real, weight_imag, power, gain)
    shares = parts.reshape(3, column_count, share_size).transpose(1, 0, 2)
    sums = jnp.sum(lax.all_to_all(shares, "col", 0, 0), axis=0)
    return sums[:2] / sums[2:]


def solution(mesh):
    return jax.shard_map(
        body,
        mesh=mesh,
        in_specs=(
            P(("chan", "col"), None, "row"),
            P(("chan", "row"), None, "col"),
            P(None, ("chan", "row", "col")),
        ),
        out_specs=P(None, ("chan", "row", "col")),
        check_vma=False,
    )
```

```python
import jax
import jax.numpy as jnp
import numpy as np
from jax import lax
from jax.experimental import pallas as pl
from jax.experimental.pallas import tpu as pltpu
from jax.sharding import PartitionSpec as P


SIDE = 4
PLANES = 8

OFFSETS = {0: (0, 0), 1: (0, 1), 2: (-1, 1), 3: (-1, 2), 4: (-2, 2)}
EARLY = [(d, h, k) for d in (1, 2) for h in (0, 1) for k in (0, 1)]
LATE = [(3, h, k) for h in (0, 1) for k in (0, 1)] + [(4, 0, 0), (4, 1, 1), (0, 0, 0), (0, 0, 1)]
PLACE = [
    [7, 0, 2, 5, 13, 10, 8, 15, 14, 6, 3, 12, 11, 9, 1, 4],
    [15, 10, 8, 2, 0, 7, 5, 13, 9, 4, 1, 14, 6, 11, 12, 3],
    [13, 8, 5, 10, 2, 0, 7, 15, 11, 14, 3, 1, 12, 9, 6, 4],
    [10, 13, 15, 2, 0, 8, 7, 5, 11, 4, 14, 9, 1, 12, 3, 6],
    [15, 8, 13, 10, 2, 5, 7, 0, 11, 6, 4, 14, 3, 1, 12, 9],
    [2, 10, 15, 0, 8, 5, 7, 13, 11, 12, 14, 9, 3, 1, 6, 4],
    [15, 0, 2, 13, 5, 8, 10, 7, 9, 14, 3, 11, 6, 4, 1, 12],
    [2, 5, 7, 10, 8, 0, 15, 13, 3, 12, 9, 1, 4, 6, 11, 14],
]


def targets(chunk, c):
    d, h, k = chunk
    a, b = [(c + offset) % PLANES for offset in OFFSETS[d]]
    if d == 0 and k == 0:
        return (2 * c, c, 0), (2 * c + 1, c, 1), 0
    if d == 0:
        return (2 * c + 1, c, 0), (2 * c, c, 1), 1
    if d == 4:
        k = h if c < PLANES // 2 else 1 - h
    plain, mirror = (2 * a + h, b, k), (2 * b + k, a, h)
    if d == 4 or h == k:
        return plain, mirror, 0
    return mirror, plain, 1


def tables():
    rows = SIDE * SIDE
    devices = rows * PLANES
    first, second = [], []
    early = np.zeros((devices, 2, SIDE, 2), np.int32)
    late = np.zeros((devices, 2, SIDE, 2), np.int32)
    ahead = np.zeros((devices, 2, SIDE), np.int32)
    flags = np.zeros((devices, 2), np.int32)
    half = np.zeros(devices, np.int32)
    for c in range(PLANES):
        for chunk, r in zip(EARLY + LATE, PLACE[c]):
            one, two, conjugated = targets(chunk, c)
            first.append((r * PLANES + c, one[0] * PLANES + one[1]))
            second.append((r * PLANES + c, two[0] * PLANES + two[1]))
            flags[r * PLANES + c] = conjugated, chunk == (0, 0, 0)
            half[one[0] * PLANES + one[1]] = one[2]
        for i, owner in enumerate(PLACE[c]):
            v, u = owner // SIDE, owner % SIDE
            order, index = (early, i) if i < len(EARLY) else (late, i - len(EARLY))
            for r in range(rows):
                y, x = r // SIDE, r % SIDE
                order[r * PLANES + c, 0, (u - x) % SIDE, v // 2] = index
                order[r * PLANES + c, 1, (v - y) % SIDE, u // 2] = index
        for r in range(rows):
            y, x = r // SIDE, r % SIDE
            for t in range(SIDE):
                v, u = (y + t) % SIDE, (x + t) % SIDE
                ahead[r * PLANES + c, 0, t] = (v + x) % 2 * 2 + v // 2
                ahead[r * PLANES + c, 1, t] = (u + y) % 2 * 2 + u // 2
    return first, second, early, late, ahead, flags, half


def matmul(lhs, rhs):
    return lax.dot_general(lhs, rhs, (((1,), (1,)), ((), ())), preferred_element_type=jnp.float32)


def rows_of(ref, half):
    quarter = ref.shape[0] // 2
    return ref[pl.ds(pl.multiple_of(half * quarter, quarter), quarter), :]


def slabs(rows, count=4):
    def run(function):
        @pl.loop(0, count)
        def _(i):
            function(pl.ds(pl.multiple_of(i * (rows // count), rows // count), rows // count))

    return run


def turn(out, block):
    times = block.shape[1] // 2

    @slabs(block.shape[0])
    def _(rows):
        out[rows, :times] = -block[rows, times:]
        out[rows, times:] = block[rows, :times]


def diagonal_kernel(block, out, turned, found):
    turn(turned, block)
    for part, rhs in enumerate((block, turned)):

        @pl.loop(0, 3)
        def _(i):
            lhs = rows_of(block, jnp.where(i == 1, 1, 0))
            found[2 * i + part] = matmul(lhs, rows_of(rhs, jnp.where(i == 0, 0, 1)))

    out[0] = found[0] + found[1]
    out[1] = found[2] + found[3]
    out[2], out[3] = found[4], found[5]


ORDER = ((2, 0), (1, 1), (2, 1), (3, 0), (1, 0), (3, 1), (0, 0), (0, 1))


def stores(right, left, up, down, own):
    return {
        (0, 0): own.at[0],
        (0, 1): own.at[1],
        (1, 0): up,
        (1, 1): right.at[1],
        (2, 0): right.at[0],
        (2, 1): left.at[0],
        (3, 0): left.at[1],
        (3, 1): down,
    }


def stack(lefts, one, two):
    @slabs(one.shape[0])
    def _(rows):
        lefts[0, rows], lefts[1, rows] = one[rows], two[rows]


def early_kernel(device, table, one, two, block, *refs):
    outs, lefts, turned = refs[:10], refs[10], refs[11]
    stack(lefts, one, two)
    turn(turned, block)
    for t, j in ORDER:
        for color, rhs in enumerate((block, turned)):
            index = table[device[0] * 16 + color * 8 + t * 2 + j]
            lhs = rows_of(lefts.at[index // 4], index // 2 % 2)
            out = stores(*outs[5 * color : 5 * color + 5])[t, j]
            out[...] = matmul(lhs, rows_of(rhs, index % 2))


def late_kernel(device, table, one, two, block, diagonal, *refs):
    outs, lefts, turned = refs[:10], refs[10], refs[11]
    stack(lefts, one, two)
    turn(turned, block)
    upper = (device[1] >= PLANES // 2).astype(jnp.int32)
    for t, j in ORDER:
        for color, rhs in enumerate((block, turned)):
            index = table[device[0] * 16 + color * 8 + t * 2 + j]
            near = index < 4
            h = jnp.where(near, index // 2, index % 2)
            k = jnp.where(near, index % 2, (h + upper) % 2)
            product = matmul(rows_of(lefts.at[index // 4], h), rows_of(rhs, k))
            ready = diagonal[jnp.maximum(index - 6, 0) * 2 + color]
            out = stores(*outs[5 * color : 5 * color + 5])[t, j]
            out[...] = jnp.where(index < 6, product, ready)


def sum_kernel(*refs):
    for color in range(2):
        own, right, left, right2, left2 = refs[5 * color : 5 * color + 5]
        refs[10 + color][0] = own[0] + right2[...] + left[0]
        refs[10 + color][1] = own[1] + right[0] + left2[...]


def finish_kernel(device, ahead, *refs):
    ins, outs, sums = refs[:12], refs[12:20], refs[20]
    for color in range(2):
        early, own, right, left, right2, left2 = ins[6 * color : 6 * color + 6]
        sums[0], sums[1] = early[0], early[1]
        sums[2] = own[0] + right2[...] + left[0]
        sums[3] = own[1] + right[0] + left2[...]
        for t in range(SIDE):
            outs[4 * color + t][...] = sums[ahead[device[0] * 8 + color * 4 + t]]


def by_slabs(kernel, scalars, parts, outs, scratch, steps=4):
    quarter = parts[0].shape[-1]
    slab = quarter // steps
    specs = {
        "one": pl.BlockSpec((slab, quarter), lambda i: (i, 0)),
        "second": pl.BlockSpec((1, slab, quarter), lambda i: (1, i, 0)),
        "both": pl.BlockSpec((2, slab, quarter), lambda i: (0, i, 0)),
    }
    pattern = ["both", "second", "second", "one", "one"]
    if len(parts) == 12:
        pattern = ["both"] + pattern
    size = {"one": (quarter, quarter), "both": (2, quarter, quarter)}
    return pl.pallas_call(
        kernel,
        grid=(steps,),
        out_shape=[jax.ShapeDtypeStruct(size[out], jnp.float32) for out in outs],
        in_specs=[pl.BlockSpec(memory_space=pltpu.SMEM)] * len(scalars) + [specs[p] for p in 2 * pattern],
        out_specs=[specs[out] for out in outs],
        scratch_shapes=[pltpu.VMEM((4, slab, quarter), jnp.float32)] * scratch,
        cost_estimate=pl.CostEstimate(
            flops=8 * quarter * quarter, bytes_accessed=72 * quarter * quarter, transcendentals=0
        ),
    )(*scalars, *parts)


def mirror_kernel(device, flags, *refs):
    p, q = [(refs[i][...] + refs[i + 2][...]) + (refs[i + 1][...] + refs[i + 3][...]) for i in (0, 4)]
    first, second = refs[8:]
    pt, qt = p.T, q.T
    flip = flags[device[0] * 2] == 1
    diagonal = flags[device[0] * 2 + 1] == 1
    first[0] = jnp.where(diagonal, 0.5 * (p + pt), jnp.where(flip, pt, p))
    first[1] = jnp.where(diagonal, 0.5 * (p - pt), jnp.where(flip, -qt, q))
    second[0] = jnp.where(diagonal, 0.5 * (q + qt), jnp.where(flip, p, pt))
    second[1] = jnp.where(diagonal, 0.5 * (q - qt), jnp.where(flip, q, -qt))


def kernel_call(kernel, scalars, blocks, shapes, flops=0, scratch=()):
    shapes = [jax.ShapeDtypeStruct(shape, jnp.float32) for shape in shapes]
    vmem = pl.BlockSpec(memory_space=pltpu.VMEM)
    smem = pl.BlockSpec(memory_space=pltpu.SMEM)
    moved = sum(v.size * v.dtype.itemsize for v in blocks) + sum(4 * v.size for v in shapes)
    return pl.pallas_call(
        kernel,
        out_shape=shapes,
        in_specs=[smem] * len(scalars) + [vmem] * len(blocks),
        out_specs=[vmem] * len(shapes),
        scratch_shapes=scratch,
        cost_estimate=pl.CostEstimate(flops=flops, bytes_accessed=moved, transcendentals=0),
    )(*scalars, *blocks)


def shift_x(value, step):
    pairs = [
        (y * SIDE + x, y * SIDE + (x + step) % SIDE) for y in range(SIDE) for x in range(SIDE)
    ]
    return lax.ppermute(value, "row", pairs)


def shift_y(value, step):
    pairs = [
        (y * SIDE + x, (y + step) % SIDE * SIDE + x) for y in range(SIDE) for x in range(SIDE)
    ]
    return lax.ppermute(value, "row", pairs)


def shift_z(value, step):
    return lax.ppermute(value, "col", [(c, (c + step) % PLANES) for c in range(PLANES)])


def ring_start(right, left, shift):
    return shift(right, 1), shift(left, -1)


def ring_sums(received, rest):
    right, left = received
    return rest[0] + right[0], rest[1] + left[0]


def ring_end(own, received, sums, shift):
    return own, *received, shift(sums[0], 1), shift(sums[1], -1)


def direct(outs, shift):
    return (outs[0],) + tuple(shift(outs[t], t) for t in range(1, SIDE))


def exchange(parts, axis):
    count = lax.axis_size(axis)
    copies = jnp.broadcast_to(parts[None], (count,) + parts.shape)
    return lax.all_to_all(copies, axis, 0, 0)


def columns_to_rows(weight_real, weight_imag, power, gain):
    real = gain[0][None, :]
    imag = gain[1][None, :]
    return jnp.stack(
        [
            jnp.sum(weight_real * real + weight_imag * imag, axis=1),
            jnp.sum(weight_real * imag - weight_imag * real, axis=1),
            jnp.sum(power * (real * real + imag * imag), axis=1),
        ]
    )


def rows_to_columns(weight_real, weight_imag, power, gain):
    real = gain[0][:, None]
    imag = gain[1][:, None]
    return jnp.stack(
        [
            jnp.sum(weight_real * real - weight_imag * imag, axis=0),
            jnp.sum(weight_real * imag + weight_imag * real, axis=0),
            jnp.sum(power * (real * real + imag * imag), axis=0),
        ]
    )


def vis_tiles(samples, gain):
    row_index = lax.axis_index("row")
    column_index = lax.axis_index("col")
    first, second, early, late, ahead, flags, half = tables()
    device_index = row_index * PLANES + column_index
    device = jnp.stack([device_index, column_index]).astype(jnp.int32)
    here = samples.reshape(samples.shape[0], -1)
    antennas, times = here.shape
    quarter = antennas // 2
    product = 2 * quarter * quarter * times
    turned = pltpu.VMEM(here.shape, here.dtype)
    stacks = pltpu.VMEM((2,) + here.shape, here.dtype), turned
    found = turned, pltpu.VMEM((6, quarter, quarter), jnp.float32)
    above, below = shift_z(here, -1), shift_z(here, 1)
    gain, above, below = lax.optimization_barrier((gain, above, below))
    above2, below2 = shift_z(above, -1), shift_z(below, 1)
    shapes = 2 * ([(2, quarter, quarter)] * 2 + [(quarter, quarter)] * 2 + [(2, quarter, quarter)])
    axes = (shift_x, shift_y)

    def chunks(kernel, table, blocks):
        scalars = device, jnp.asarray(table.reshape(-1))
        return kernel_call(kernel, scalars, blocks, shapes, 16 * product, stacks)

    outs = chunks(early_kernel, early, (here, below, above))
    received = [ring_start(*outs[5 * i : 5 * i + 2], axes[i]) for i in range(2)]
    (diagonal,) = kernel_call(
        diagonal_kernel, (), (here,), [(4, quarter, quarter)], 6 * product, found
    )
    sums = [ring_sums(received[i], outs[5 * i + 2 : 5 * i + 4]) for i in range(2)]
    early_parts = [ring_end(outs[5 * i + 4], received[i], sums[i], axes[i]) for i in range(2)]
    early_total = by_slabs(sum_kernel, (), early_parts[0] + early_parts[1], ["both"] * 2, 0)
    outs = chunks(late_kernel, late, (below, below2, above2, diagonal))
    received = [ring_start(*outs[5 * i : 5 * i + 2], axes[i]) for i in range(2)]
    sums = [ring_sums(received[i], outs[5 * i + 2 : 5 * i + 4]) for i in range(2)]
    late_parts = [ring_end(outs[5 * i + 4], received[i], sums[i], axes[i]) for i in range(2)]
    outs = by_slabs(
        finish_kernel,
        (device, jnp.asarray(ahead.reshape(-1))),
        (early_total[0], *late_parts[0], early_total[1], *late_parts[1]),
        ["one"] * 8,
        1,
    )
    parts = direct(outs[:4], shift_y) + direct(outs[4:], shift_x)
    one, two = kernel_call(
        mirror_kernel,
        (device, jnp.asarray(flags.reshape(-1))),
        parts,
        [(2, quarter, quarter)] * 2,
    )
    one = lax.ppermute(one, ("row", "col"), first)
    two = lax.ppermute(two, ("row", "col"), second)
    one_is_right = jnp.asarray(half)[device_index] == 1
    left = jnp.where(one_is_right, two, one)
    right = jnp.where(one_is_right, one, two)
    real = jnp.concatenate([left[0], right[0]], axis=1)
    imag = jnp.concatenate([left[1], right[1]], axis=1)
    return real, imag, gain


def starting_gains(initial_gains):
    blocks = SIDE * SIDE // PLANES
    pairs = [
        (r * PLANES + c, (r % blocks * PLANES + c) * PLANES + r // blocks)
        for r in range(SIDE * SIDE)
        for c in range(PLANES)
    ]
    share = lax.ppermute(initial_gains, ("row", "col"), pairs)
    return exchange(share, "row").transpose(1, 0, 2).reshape(2, -1)


def body(samples, sky_model, initial_gains):
    row_count = lax.axis_size("row")
    column_count = lax.axis_size("col")
    row_index = lax.axis_index("row")
    column_index = lax.axis_index("col")
    block_column = samples.shape[0]
    block_row = sky_model.shape[0]
    share_size = initial_gains.shape[1]
    blocks = block_column // block_row
    gain = starting_gains(initial_gains)
    vis_real, vis_imag, gain = vis_tiles(samples, gain)
    model_real = sky_model[:, 0, :].astype(jnp.float32)
    model_imag = sky_model[:, 1, :].astype(jnp.float32)
    global_rows = row_index * block_row + lax.broadcasted_iota(
        jnp.int32, (block_row, block_column), 0
    )
    global_columns = column_index * block_column + lax.broadcasted_iota(
        jnp.int32, (block_row, block_column), 1
    )
    cross_mask = (global_rows != global_columns).astype(jnp.float32)
    weight_real = (vis_real * model_real + vis_imag * model_imag) * cross_mask
    weight_imag = (vis_real * model_imag - vis_imag * model_real) * cross_mask
    power = (model_real * model_real + model_imag * model_imag) * cross_mask

    parts = columns_to_rows(weight_real, weight_imag, power, gain)
    sums = jnp.sum(exchange(parts.reshape(-1, 128), "col"), axis=0).reshape(parts.shape)
    gain = sums[:2] / sums[2:]

    parts = rows_to_columns(weight_real, weight_imag, power, gain)
    message = jnp.concatenate([parts.reshape(-1), gain.reshape(-1)])
    message = message.reshape(-1, 128)
    received = exchange(message, "row").reshape(row_count, -1)
    sums = jnp.sum(received[:, : 3 * block_column], axis=0).reshape(3, block_column)
    previous = lax.dynamic_slice_in_dim(
        received[:, 3 * block_column :], column_index * blocks, blocks, 0
    )
    previous = previous.reshape(blocks, 2, block_row).transpose(1, 0, 2).reshape(2, block_column)
    gain = 0.5 * (sums[:2] / sums[2:] + previous)

    parts = columns_to_rows(weight_real, weight_imag, power, gain)
    shares = parts.reshape(3, column_count, share_size).transpose(1, 0, 2)
    sums = jnp.sum(lax.all_to_all(shares, "col", 0, 0), axis=0)
    return sums[:2] / sums[2:]


def solution(mesh):
    return jax.shard_map(
        body,
        mesh=mesh,
        in_specs=(
            P(("chan", "col"), None, "row"),
            P(("chan", "row"), None, "col"),
            P(None, ("chan", "row", "col")),
        ),
        out_specs=P(None, ("chan", "row", "col")),
        check_vma=False,
    )
```

```python
import jax
import jax.numpy as jnp
import numpy as np
from jax import lax
from jax.experimental import pallas as pl
from jax.experimental.pallas import tpu as pltpu
from jax.sharding import PartitionSpec as P


SIDE = 4
PLANES = 8

OFFSETS = {0: (0, 0), 1: (0, 1), 2: (-1, 1), 3: (-1, 2), 4: (-2, 2)}
EARLY = [(d, h, k) for d in (1, 2) for h in (0, 1) for k in (0, 1)]
LATE = [(3, h, k) for h in (0, 1) for k in (0, 1)] + [(4, 0, 0), (4, 1, 1), (0, 0, 0), (0, 0, 1)]
PLACE = [
    [7, 0, 2, 5, 13, 10, 8, 15, 14, 6, 3, 12, 11, 9, 1, 4],
    [15, 10, 8, 2, 0, 7, 5, 13, 9, 4, 1, 14, 6, 11, 12, 3],
    [13, 8, 5, 10, 2, 0, 7, 15, 11, 14, 3, 1, 12, 9, 6, 4],
    [10, 13, 15, 2, 0, 8, 7, 5, 11, 4, 14, 9, 1, 12, 3, 6],
    [15, 8, 13, 10, 2, 5, 7, 0, 11, 6, 4, 14, 3, 1, 12, 9],
    [2, 10, 15, 0, 8, 5, 7, 13, 11, 12, 14, 9, 3, 1, 6, 4],
    [15, 0, 2, 13, 5, 8, 10, 7, 9, 14, 3, 11, 6, 4, 1, 12],
    [2, 5, 7, 10, 8, 0, 15, 13, 3, 12, 9, 1, 4, 6, 11, 14],
]


def targets(chunk, c):
    d, h, k = chunk
    a, b = [(c + offset) % PLANES for offset in OFFSETS[d]]
    if d == 0 and k == 0:
        return (2 * c, c, 0), (2 * c + 1, c, 1), 0
    if d == 0:
        return (2 * c + 1, c, 0), (2 * c, c, 1), 1
    if d == 4:
        k = h if c < PLANES // 2 else 1 - h
    plain, mirror = (2 * a + h, b, k), (2 * b + k, a, h)
    if d == 4 or h == k:
        return plain, mirror, 0
    return mirror, plain, 1


def tables():
    rows = SIDE * SIDE
    devices = rows * PLANES
    first, second = [], []
    early = np.zeros((devices, 2, SIDE, 2), np.int32)
    late = np.zeros((devices, 2, SIDE, 2), np.int32)
    ahead = np.zeros((devices, 2, SIDE), np.int32)
    flags = np.zeros((devices, 2), np.int32)
    half = np.zeros(devices, np.int32)
    for c in range(PLANES):
        for chunk, r in zip(EARLY + LATE, PLACE[c]):
            one, two, conjugated = targets(chunk, c)
            first.append((r * PLANES + c, one[0] * PLANES + one[1]))
            second.append((r * PLANES + c, two[0] * PLANES + two[1]))
            flags[r * PLANES + c] = conjugated, chunk == (0, 0, 0)
            half[one[0] * PLANES + one[1]] = one[2]
        for i, owner in enumerate(PLACE[c]):
            v, u = owner // SIDE, owner % SIDE
            order, index = (early, i) if i < len(EARLY) else (late, i - len(EARLY))
            for r in range(rows):
                y, x = r // SIDE, r % SIDE
                order[r * PLANES + c, 0, (u - x) % SIDE, v // 2] = index
                order[r * PLANES + c, 1, (v - y) % SIDE, u // 2] = index
        for r in range(rows):
            y, x = r // SIDE, r % SIDE
            for t in range(SIDE):
                v, u = (y + t) % SIDE, (x + t) % SIDE
                ahead[r * PLANES + c, 0, t] = (v + x) % 2 * 2 + v // 2
                ahead[r * PLANES + c, 1, t] = (u + y) % 2 * 2 + u // 2
    return first, second, early, late, ahead, flags, half


def matmul(lhs, rhs):
    return lax.dot_general(lhs, rhs, (((1,), (1,)), ((), ())), preferred_element_type=jnp.float32)


def rows_of(ref, half):
    quarter = ref.shape[0] // 2
    return ref[pl.ds(pl.multiple_of(half * quarter, quarter), quarter), :]


def slabs(rows, count=4):
    def run(function):
        @pl.loop(0, count)
        def _(i):
            function(pl.ds(pl.multiple_of(i * (rows // count), rows // count), rows // count))

    return run


def turn(out, block):
    times = block.shape[1] // 2

    @slabs(block.shape[0])
    def _(rows):
        out[rows, :times] = -block[rows, times:]
        out[rows, times:] = block[rows, :times]


def diagonal_kernel(block, out, turned, found):
    turn(turned, block)
    for part, rhs in enumerate((block, turned)):

        @pl.loop(0, 3)
        def _(i):
            lhs = rows_of(block, jnp.where(i == 1, 1, 0))
            found[2 * i + part] = matmul(lhs, rows_of(rhs, jnp.where(i == 0, 0, 1)))

    out[0] = found[0] + found[1]
    out[1] = found[2] + found[3]
    out[2], out[3] = found[4], found[5]


ORDER = ((2, 0), (1, 1), (2, 1), (3, 0), (1, 0), (3, 1), (0, 0), (0, 1))


def stores(right, left, up, down, own):
    return {
        (0, 0): own.at[0],
        (0, 1): own.at[1],
        (1, 0): up,
        (1, 1): right.at[1],
        (2, 0): right.at[0],
        (2, 1): left.at[0],
        (3, 0): left.at[1],
        (3, 1): down,
    }


def stack(lefts, one, two):
    @slabs(one.shape[0])
    def _(rows):
        lefts[0, rows], lefts[1, rows] = one[rows], two[rows]


def early_kernel(device, table, one, two, block, *refs):
    outs, lefts, turned = refs[:8], refs[8], refs[9]
    stack(lefts, one, two)
    turn(turned, block)
    for t, j in ORDER:
        for color, rhs in enumerate((block, turned)):
            index = table[device[0] * 16 + color * 8 + t * 2 + j]
            lhs = rows_of(lefts.at[index // 4], index // 2 % 2)
            outs[4 * color + t][j] = matmul(lhs, rows_of(rhs, index % 2))


def late_kernel(device, table, one, two, block, diagonal, *refs):
    outs, lefts, turned = refs[:10], refs[10], refs[11]
    stack(lefts, one, two)
    turn(turned, block)
    upper = (device[1] >= PLANES // 2).astype(jnp.int32)
    for t, j in ORDER:
        for color, rhs in enumerate((block, turned)):
            index = table[device[0] * 16 + color * 8 + t * 2 + j]
            near = index < 4
            h = jnp.where(near, index // 2, index % 2)
            k = jnp.where(near, index % 2, (h + upper) % 2)
            product = matmul(rows_of(lefts.at[index // 4], h), rows_of(rhs, k))
            ready = diagonal[jnp.maximum(index - 6, 0) * 2 + color]
            out = stores(*outs[5 * color : 5 * color + 5])[t, j]
            out[...] = jnp.where(index < 6, product, ready)


def sum_kernel(*refs):
    for color in range(2):
        own, one, two, three = refs[4 * color : 4 * color + 4]
        refs[8 + color][...] = (own[...] + one[...]) + (two[...] + three[...])


def finish_kernel(device, ahead, *refs):
    ins, outs, sums = refs[:12], refs[12:20], refs[20]
    for color in range(2):
        early, own, right, left, right2, left2 = ins[6 * color : 6 * color + 6]
        sums[0], sums[1] = early[0], early[1]
        sums[2] = own[0] + right2[...] + left[0]
        sums[3] = own[1] + right[0] + left2[...]
        for t in range(SIDE):
            outs[4 * color + t][...] = sums[ahead[device[0] * 8 + color * 4 + t]]


def by_slabs(kernel, scalars, parts, outs, scratch, steps=4):
    quarter = parts[0].shape[-1]
    slab = quarter // steps
    specs = {
        "one": pl.BlockSpec((slab, quarter), lambda i: (i, 0)),
        "second": pl.BlockSpec((1, slab, quarter), lambda i: (1, i, 0)),
        "both": pl.BlockSpec((2, slab, quarter), lambda i: (0, i, 0)),
    }
    pattern = ["both"] * 4 if len(parts) == 8 else ["both", "both", "second", "second", "one", "one"]
    size = {"one": (quarter, quarter), "both": (2, quarter, quarter)}
    return pl.pallas_call(
        kernel,
        grid=(steps,),
        out_shape=[jax.ShapeDtypeStruct(size[out], jnp.float32) for out in outs],
        in_specs=[pl.BlockSpec(memory_space=pltpu.SMEM)] * len(scalars) + [specs[p] for p in 2 * pattern],
        out_specs=[specs[out] for out in outs],
        scratch_shapes=[pltpu.VMEM((4, slab, quarter), jnp.float32)] * scratch,
        cost_estimate=pl.CostEstimate(
            flops=8 * quarter * quarter, bytes_accessed=72 * quarter * quarter, transcendentals=0
        ),
    )(*scalars, *parts)


def mirror_kernel(device, flags, *refs):
    p, q = [(refs[i][...] + refs[i + 2][...]) + (refs[i + 1][...] + refs[i + 3][...]) for i in (0, 4)]
    first, second = refs[8:]
    pt, qt = p.T, q.T
    flip = flags[device[0] * 2] == 1
    diagonal = flags[device[0] * 2 + 1] == 1
    first[0] = jnp.where(diagonal, 0.5 * (p + pt), jnp.where(flip, pt, p))
    first[1] = jnp.where(diagonal, 0.5 * (p - pt), jnp.where(flip, -qt, q))
    second[0] = jnp.where(diagonal, 0.5 * (q + qt), jnp.where(flip, p, pt))
    second[1] = jnp.where(diagonal, 0.5 * (q - qt), jnp.where(flip, q, -qt))


def kernel_call(kernel, scalars, blocks, shapes, flops=0, scratch=()):
    shapes = [jax.ShapeDtypeStruct(shape, jnp.float32) for shape in shapes]
    vmem = pl.BlockSpec(memory_space=pltpu.VMEM)
    smem = pl.BlockSpec(memory_space=pltpu.SMEM)
    moved = sum(v.size * v.dtype.itemsize for v in blocks) + sum(4 * v.size for v in shapes)
    return pl.pallas_call(
        kernel,
        out_shape=shapes,
        in_specs=[smem] * len(scalars) + [vmem] * len(blocks),
        out_specs=[vmem] * len(shapes),
        scratch_shapes=scratch,
        cost_estimate=pl.CostEstimate(flops=flops, bytes_accessed=moved, transcendentals=0),
    )(*scalars, *blocks)


def shift_x(value, step):
    pairs = [
        (y * SIDE + x, y * SIDE + (x + step) % SIDE) for y in range(SIDE) for x in range(SIDE)
    ]
    return lax.ppermute(value, "row", pairs)


def shift_y(value, step):
    pairs = [
        (y * SIDE + x, (y + step) % SIDE * SIDE + x) for y in range(SIDE) for x in range(SIDE)
    ]
    return lax.ppermute(value, "row", pairs)


def shift_z(value, step):
    return lax.ppermute(value, "col", [(c, (c + step) % PLANES) for c in range(PLANES)])


def ring_start(right, left, shift):
    return shift(right, 1), shift(left, -1)


def ring_sums(received, rest):
    right, left = received
    return rest[0] + right[0], rest[1] + left[0]


def ring_end(own, received, sums, shift):
    return own, *received, shift(sums[0], 1), shift(sums[1], -1)


def direct(outs, shift):
    far = shift(outs[2], 2)
    return outs[0], shift(outs[1], 1), far, shift(outs[3], 3)


def exchange(parts, axis):
    count = lax.axis_size(axis)
    copies = jnp.broadcast_to(parts[None], (count,) + parts.shape)
    return lax.all_to_all(copies, axis, 0, 0)


def columns_to_rows(weight_real, weight_imag, power, gain):
    real = gain[0][None, :]
    imag = gain[1][None, :]
    return jnp.stack(
        [
            jnp.sum(weight_real * real + weight_imag * imag, axis=1),
            jnp.sum(weight_real * imag - weight_imag * real, axis=1),
            jnp.sum(power * (real * real + imag * imag), axis=1),
        ]
    )


def rows_to_columns(weight_real, weight_imag, power, gain):
    real = gain[0][:, None]
    imag = gain[1][:, None]
    return jnp.stack(
        [
            jnp.sum(weight_real * real - weight_imag * imag, axis=0),
            jnp.sum(weight_real * imag + weight_imag * real, axis=0),
            jnp.sum(power * (real * real + imag * imag), axis=0),
        ]
    )


def vis_tiles(samples, gain):
    row_index = lax.axis_index("row")
    column_index = lax.axis_index("col")
    first, second, early, late, ahead, flags, half = tables()
    device_index = row_index * PLANES + column_index
    device = jnp.stack([device_index, column_index]).astype(jnp.int32)
    here = samples.reshape(samples.shape[0], -1)
    antennas, times = here.shape
    quarter = antennas // 2
    product = 2 * quarter * quarter * times
    turned = pltpu.VMEM(here.shape, here.dtype)
    stacks = pltpu.VMEM((2,) + here.shape, here.dtype), turned
    found = turned, pltpu.VMEM((6, quarter, quarter), jnp.float32)
    above, below = shift_z(here, -1), shift_z(here, 1)
    gain, above, below = lax.optimization_barrier((gain, above, below))
    above2, below2 = shift_z(above, -1), shift_z(below, 1)
    shapes = 2 * ([(2, quarter, quarter)] * 2 + [(quarter, quarter)] * 2 + [(2, quarter, quarter)])
    axes = (shift_x, shift_y)

    def chunks(kernel, table, blocks, shapes):
        scalars = device, jnp.asarray(table.reshape(-1))
        return kernel_call(kernel, scalars, blocks, shapes, 16 * product, stacks)

    outs = chunks(early_kernel, early, (here, below, above), [(2, quarter, quarter)] * 8)
    early_parts = [direct(outs[4 * i : 4 * i + 4], axes[i]) for i in range(2)]
    (diagonal,) = kernel_call(
        diagonal_kernel, (), (here,), [(4, quarter, quarter)], 6 * product, found
    )
    early_total = by_slabs(sum_kernel, (), early_parts[0] + early_parts[1], ["both"] * 2, 0)
    outs = chunks(late_kernel, late, (below, below2, above2, diagonal), shapes)
    received = [ring_start(*outs[5 * i : 5 * i + 2], axes[i]) for i in range(2)]
    sums = [ring_sums(received[i], outs[5 * i + 2 : 5 * i + 4]) for i in range(2)]
    late_parts = [ring_end(outs[5 * i + 4], received[i], sums[i], axes[i]) for i in range(2)]
    outs = by_slabs(
        finish_kernel,
        (device, jnp.asarray(ahead.reshape(-1))),
        (early_total[0], *late_parts[0], early_total[1], *late_parts[1]),
        ["one"] * 8,
        1,
    )
    parts = direct(outs[:4], shift_y) + direct(outs[4:], shift_x)
    one, two = kernel_call(
        mirror_kernel,
        (device, jnp.asarray(flags.reshape(-1))),
        parts,
        [(2, quarter, quarter)] * 2,
    )
    one = lax.ppermute(one, ("row", "col"), first)
    two = lax.ppermute(two, ("row", "col"), second)
    one_is_right = jnp.asarray(half)[device_index] == 1
    left = jnp.where(one_is_right, two, one)
    right = jnp.where(one_is_right, one, two)
    real = jnp.concatenate([left[0], right[0]], axis=1)
    imag = jnp.concatenate([left[1], right[1]], axis=1)
    return real, imag, gain


def starting_gains(initial_gains):
    blocks = SIDE * SIDE // PLANES
    pairs = [
        (r * PLANES + c, (r % blocks * PLANES + c) * PLANES + r // blocks)
        for r in range(SIDE * SIDE)
        for c in range(PLANES)
    ]
    share = lax.ppermute(initial_gains, ("row", "col"), pairs)
    return exchange(share, "row").transpose(1, 0, 2).reshape(2, -1)


def body(samples, sky_model, initial_gains):
    row_count = lax.axis_size("row")
    column_count = lax.axis_size("col")
    row_index = lax.axis_index("row")
    column_index = lax.axis_index("col")
    block_column = samples.shape[0]
    block_row = sky_model.shape[0]
    share_size = initial_gains.shape[1]
    blocks = block_column // block_row
    gain = starting_gains(initial_gains)
    vis_real, vis_imag, gain = vis_tiles(samples, gain)
    model_real = sky_model[:, 0, :].astype(jnp.float32)
    model_imag = sky_model[:, 1, :].astype(jnp.float32)
    global_rows = row_index * block_row + lax.broadcasted_iota(
        jnp.int32, (block_row, block_column), 0
    )
    global_columns = column_index * block_column + lax.broadcasted_iota(
        jnp.int32, (block_row, block_column), 1
    )
    cross_mask = (global_rows != global_columns).astype(jnp.float32)
    weight_real = (vis_real * model_real + vis_imag * model_imag) * cross_mask
    weight_imag = (vis_real * model_imag - vis_imag * model_real) * cross_mask
    power = (model_real * model_real + model_imag * model_imag) * cross_mask

    parts = columns_to_rows(weight_real, weight_imag, power, gain)
    sums = jnp.sum(exchange(parts.reshape(-1, 128), "col"), axis=0).reshape(parts.shape)
    gain = sums[:2] / sums[2:]

    parts = rows_to_columns(weight_real, weight_imag, power, gain)
    message = jnp.concatenate([parts.reshape(-1), gain.reshape(-1)])
    message = message.reshape(-1, 128)
    received = exchange(message, "row").reshape(row_count, -1)
    sums = jnp.sum(received[:, : 3 * block_column], axis=0).reshape(3, block_column)
    previous = lax.dynamic_slice_in_dim(
        received[:, 3 * block_column :], column_index * blocks, blocks, 0
    )
    previous = previous.reshape(blocks, 2, block_row).transpose(1, 0, 2).reshape(2, block_column)
    gain = 0.5 * (sums[:2] / sums[2:] + previous)

    parts = columns_to_rows(weight_real, weight_imag, power, gain)
    shares = parts.reshape(3, column_count, share_size).transpose(1, 0, 2)
    sums = jnp.sum(lax.all_to_all(shares, "col", 0, 0), axis=0)
    return sums[:2] / sums[2:]


def solution(mesh):
    return jax.shard_map(
        body,
        mesh=mesh,
        in_specs=(
            P(("chan", "col"), None, "row"),
            P(("chan", "row"), None, "col"),
            P(None, ("chan", "row", "col")),
        ),
        out_specs=P(None, ("chan", "row", "col")),
        check_vma=False,
    )
```

```python
import jax
import jax.numpy as jnp
import numpy as np
from jax import lax
from jax.experimental import pallas as pl
from jax.experimental.pallas import tpu as pltpu
from jax.sharding import PartitionSpec as P


SIDE = 4
PLANES = 8

OFFSETS = {0: (0, 0), 1: (0, 1), 2: (-1, 1), 3: (-1, 2), 4: (-2, 2)}
EARLY = [(d, h, k) for d in (1, 2) for h in (0, 1) for k in (0, 1)]
LATE = [(3, h, k) for h in (0, 1) for k in (0, 1)] + [(4, 0, 0), (4, 1, 1), (0, 0, 0), (0, 0, 1)]
PLACE = [
    [7, 0, 2, 5, 13, 10, 8, 15, 14, 6, 3, 12, 11, 9, 1, 4],
    [15, 10, 8, 2, 0, 7, 5, 13, 9, 4, 1, 14, 6, 11, 12, 3],
    [13, 8, 5, 10, 2, 0, 7, 15, 11, 14, 3, 1, 12, 9, 6, 4],
    [10, 13, 15, 2, 0, 8, 7, 5, 11, 4, 14, 9, 1, 12, 3, 6],
    [15, 8, 13, 10, 2, 5, 7, 0, 11, 6, 4, 14, 3, 1, 12, 9],
    [2, 10, 15, 0, 8, 5, 7, 13, 11, 12, 14, 9, 3, 1, 6, 4],
    [15, 0, 2, 13, 5, 8, 10, 7, 9, 14, 3, 11, 6, 4, 1, 12],
    [2, 5, 7, 10, 8, 0, 15, 13, 3, 12, 9, 1, 4, 6, 11, 14],
]


def targets(chunk, c):
    d, h, k = chunk
    a, b = [(c + offset) % PLANES for offset in OFFSETS[d]]
    if d == 0 and k == 0:
        return (2 * c, c, 0), (2 * c + 1, c, 1), 0
    if d == 0:
        return (2 * c + 1, c, 0), (2 * c, c, 1), 1
    if d == 4:
        k = h if c < PLANES // 2 else 1 - h
    plain, mirror = (2 * a + h, b, k), (2 * b + k, a, h)
    if d == 4 or h == k:
        return plain, mirror, 0
    return mirror, plain, 1


def tables():
    rows = SIDE * SIDE
    devices = rows * PLANES
    first, second = [], []
    early = np.zeros((devices, 2, SIDE, 2), np.int32)
    late = np.zeros((devices, 2, SIDE, 2), np.int32)
    ahead = np.zeros((devices, 2, SIDE), np.int32)
    flags = np.zeros((devices, 2), np.int32)
    half = np.zeros(devices, np.int32)
    for c in range(PLANES):
        for chunk, r in zip(EARLY + LATE, PLACE[c]):
            one, two, conjugated = targets(chunk, c)
            first.append((r * PLANES + c, one[0] * PLANES + one[1]))
            second.append((r * PLANES + c, two[0] * PLANES + two[1]))
            flags[r * PLANES + c] = conjugated, chunk == (0, 0, 0)
            half[one[0] * PLANES + one[1]] = one[2]
        for i, owner in enumerate(PLACE[c]):
            v, u = owner // SIDE, owner % SIDE
            order, index = (early, i) if i < len(EARLY) else (late, i - len(EARLY))
            for r in range(rows):
                y, x = r // SIDE, r % SIDE
                order[r * PLANES + c, 0, (u - x) % SIDE, v // 2] = index
                order[r * PLANES + c, 1, (v - y) % SIDE, u // 2] = index
        for r in range(rows):
            y, x = r // SIDE, r % SIDE
            for t in range(SIDE):
                v, u = (y + t) % SIDE, (x + t) % SIDE
                ahead[r * PLANES + c, 0, t] = (v + x) % 2 * 2 + v // 2
                ahead[r * PLANES + c, 1, t] = (u + y) % 2 * 2 + u // 2
    return first, second, early, late, ahead, flags, half


def matmul(lhs, rhs):
    return lax.dot_general(lhs, rhs, (((1,), (1,)), ((), ())), preferred_element_type=jnp.float32)


def rows_of(ref, half):
    quarter = ref.shape[0] // 2
    return ref[pl.ds(pl.multiple_of(half * quarter, quarter), quarter), :]


def slabs(rows, count=4):
    def run(function):
        @pl.loop(0, count)
        def _(i):
            function(pl.ds(pl.multiple_of(i * (rows // count), rows // count), rows // count))

    return run


def turn(out, block):
    times = block.shape[1] // 2

    @slabs(block.shape[0])
    def _(rows):
        out[rows, :times] = -block[rows, times:]
        out[rows, times:] = block[rows, :times]


def diagonal_kernel(block, out, turned, found):
    turn(turned, block)
    for part, rhs in enumerate((block, turned)):

        @pl.loop(0, 3)
        def _(i):
            lhs = rows_of(block, jnp.where(i == 1, 1, 0))
            found[2 * i + part] = matmul(lhs, rows_of(rhs, jnp.where(i == 0, 0, 1)))

    out[0] = found[0] + found[1]
    out[1] = found[2] + found[3]
    out[2], out[3] = found[4], found[5]


ORDER = ((2, 0), (1, 1), (2, 1), (3, 0), (1, 0), (3, 1), (0, 0), (0, 1))


def stores(right, left, up, down, own):
    return {
        (0, 0): own.at[0],
        (0, 1): own.at[1],
        (1, 0): up,
        (1, 1): right.at[1],
        (2, 0): right.at[0],
        (2, 1): left.at[0],
        (3, 0): left.at[1],
        (3, 1): down,
    }


def stack(lefts, one, two):
    @slabs(one.shape[0])
    def _(rows):
        lefts[0, rows], lefts[1, rows] = one[rows], two[rows]


def early_kernel(device, table, one, two, block, *refs):
    outs, lefts, turned = refs[:10], refs[10], refs[11]
    stack(lefts, one, two)
    turn(turned, block)
    for t, j in ORDER:
        for color, rhs in enumerate((block, turned)):
            index = table[device[0] * 16 + color * 8 + t * 2 + j]
            lhs = rows_of(lefts.at[index // 4], index // 2 % 2)
            out = stores(*outs[5 * color : 5 * color + 5])[t, j]
            out[...] = matmul(lhs, rows_of(rhs, index % 2))


def late_kernel(device, table, one, two, block, diagonal, *refs):
    outs, lefts, turned = refs[:10], refs[10], refs[11]
    stack(lefts, one, two)
    turn(turned, block)
    upper = (device[1] >= PLANES // 2).astype(jnp.int32)
    for t, j in ORDER:
        for color, rhs in enumerate((block, turned)):
            index = table[device[0] * 16 + color * 8 + t * 2 + j]
            near = index < 4
            h = jnp.where(near, index // 2, index % 2)
            k = jnp.where(near, index % 2, (h + upper) % 2)
            product = matmul(rows_of(lefts.at[index // 4], h), rows_of(rhs, k))
            ready = diagonal[jnp.maximum(index - 6, 0) * 2 + color]
            out = stores(*outs[5 * color : 5 * color + 5])[t, j]
            out[...] = jnp.where(index < 6, product, ready)


def sum_kernel(*refs):
    for color in range(2):
        own, right, left, right2, left2 = refs[5 * color : 5 * color + 5]
        refs[10 + color][0] = own[0] + right2[...] + left[0]
        refs[10 + color][1] = own[1] + right[0] + left2[...]


def finish_kernel(device, ahead, *refs):
    ins, outs, sums = refs[:12], refs[12:20], refs[20]
    for color in range(2):
        early, own, right, left, right2, left2 = ins[6 * color : 6 * color + 6]
        sums[0], sums[1] = early[0], early[1]
        sums[2] = own[0] + right2[...] + left[0]
        sums[3] = own[1] + right[0] + left2[...]
        for t in range(SIDE):
            outs[4 * color + t][...] = sums[ahead[device[0] * 8 + color * 4 + t]]


def by_slabs(kernel, scalars, parts, outs, scratch, steps=4):
    quarter = parts[0].shape[-1]
    slab = quarter // steps
    specs = {
        "one": pl.BlockSpec((slab, quarter), lambda i: (i, 0)),
        "second": pl.BlockSpec((1, slab, quarter), lambda i: (1, i, 0)),
        "both": pl.BlockSpec((2, slab, quarter), lambda i: (0, i, 0)),
    }
    pattern = ["both", "second", "second", "one", "one"]
    if len(parts) == 12:
        pattern = ["both"] + pattern
    size = {"one": (quarter, quarter), "both": (2, quarter, quarter)}
    return pl.pallas_call(
        kernel,
        grid=(steps,),
        out_shape=[jax.ShapeDtypeStruct(size[out], jnp.float32) for out in outs],
        in_specs=[pl.BlockSpec(memory_space=pltpu.SMEM)] * len(scalars) + [specs[p] for p in 2 * pattern],
        out_specs=[specs[out] for out in outs],
        scratch_shapes=[pltpu.VMEM((4, slab, quarter), jnp.float32)] * scratch,
        cost_estimate=pl.CostEstimate(
            flops=8 * quarter * quarter, bytes_accessed=72 * quarter * quarter, transcendentals=0
        ),
    )(*scalars, *parts)


def mirror_kernel(device, flags, *refs):
    p, q = [(refs[i][...] + refs[i + 2][...]) + (refs[i + 1][...] + refs[i + 3][...]) for i in (0, 4)]
    first, second = refs[8:]
    pt, qt = p.T, q.T
    flip = flags[device[0] * 2] == 1
    diagonal = flags[device[0] * 2 + 1] == 1
    first[0] = jnp.where(diagonal, 0.5 * (p + pt), jnp.where(flip, pt, p))
    first[1] = jnp.where(diagonal, 0.5 * (p - pt), jnp.where(flip, -qt, q))
    second[0] = jnp.where(diagonal, 0.5 * (q + qt), jnp.where(flip, p, pt))
    second[1] = jnp.where(diagonal, 0.5 * (q - qt), jnp.where(flip, q, -qt))


def kernel_call(kernel, scalars, blocks, shapes, flops=0, scratch=()):
    shapes = [jax.ShapeDtypeStruct(shape, jnp.float32) for shape in shapes]
    vmem = pl.BlockSpec(memory_space=pltpu.VMEM)
    smem = pl.BlockSpec(memory_space=pltpu.SMEM)
    moved = sum(v.size * v.dtype.itemsize for v in blocks) + sum(4 * v.size for v in shapes)
    return pl.pallas_call(
        kernel,
        out_shape=shapes,
        in_specs=[smem] * len(scalars) + [vmem] * len(blocks),
        out_specs=[vmem] * len(shapes),
        scratch_shapes=scratch,
        cost_estimate=pl.CostEstimate(flops=flops, bytes_accessed=moved, transcendentals=0),
    )(*scalars, *blocks)


def shift_x(value, step):
    pairs = [
        (y * SIDE + x, y * SIDE + (x + step) % SIDE) for y in range(SIDE) for x in range(SIDE)
    ]
    return lax.ppermute(value, "row", pairs)


def shift_y(value, step):
    pairs = [
        (y * SIDE + x, (y + step) % SIDE * SIDE + x) for y in range(SIDE) for x in range(SIDE)
    ]
    return lax.ppermute(value, "row", pairs)


def shift_z(value, step):
    return lax.ppermute(value, "col", [(c, (c + step) % PLANES) for c in range(PLANES)])


def ring_start(right, left, shift):
    return shift(right, 1), shift(left, -1)


def ring_sums(received, rest):
    right, left = received
    return rest[0] + right[0], rest[1] + left[0]


def ring_end(own, received, sums, shift):
    return own, *received, shift(sums[0], 1), shift(sums[1], -1)


def direct(outs, shift):
    return (outs[0],) + tuple(shift(outs[t], t) for t in range(1, SIDE))


def exchange(parts, axis):
    count = lax.axis_size(axis)
    copies = jnp.broadcast_to(parts[None], (count,) + parts.shape)
    return lax.all_to_all(copies, axis, 0, 0)


def columns_to_rows(weight_real, weight_imag, power, gain):
    real = gain[0][None, :]
    imag = gain[1][None, :]
    return jnp.stack(
        [
            jnp.sum(weight_real * real + weight_imag * imag, axis=1),
            jnp.sum(weight_real * imag - weight_imag * real, axis=1),
            jnp.sum(power * (real * real + imag * imag), axis=1),
        ]
    )


def rows_to_columns(weight_real, weight_imag, power, gain):
    real = gain[0][:, None]
    imag = gain[1][:, None]
    return jnp.stack(
        [
            jnp.sum(weight_real * real - weight_imag * imag, axis=0),
            jnp.sum(weight_real * imag + weight_imag * real, axis=0),
            jnp.sum(power * (real * real + imag * imag), axis=0),
        ]
    )


def vis_tiles(samples, gain):
    row_index = lax.axis_index("row")
    column_index = lax.axis_index("col")
    first, second, early, late, ahead, flags, half = tables()
    device_index = row_index * PLANES + column_index
    device = jnp.stack([device_index, column_index]).astype(jnp.int32)
    here = samples.reshape(samples.shape[0], -1)
    antennas, times = here.shape
    quarter = antennas // 2
    product = 2 * quarter * quarter * times
    turned = pltpu.VMEM(here.shape, here.dtype)
    stacks = pltpu.VMEM((2,) + here.shape, here.dtype), turned
    found = turned, pltpu.VMEM((6, quarter, quarter), jnp.float32)
    above, below = shift_z(here, -1), shift_z(here, 1)
    gain, above, below = lax.optimization_barrier((gain, above, below))
    above2, below2 = shift_z(above, -1), shift_z(below, 1)
    shapes = 2 * ([(2, quarter, quarter)] * 2 + [(quarter, quarter)] * 2 + [(2, quarter, quarter)])
    axes = (shift_x, shift_y)

    def chunks(kernel, table, blocks):
        scalars = device, jnp.asarray(table.reshape(-1))
        return kernel_call(kernel, scalars, blocks, shapes, 16 * product, stacks)

    outs = chunks(early_kernel, early, (here, below, above))
    received = [ring_start(*outs[5 * i : 5 * i + 2], axes[i]) for i in range(2)]
    (diagonal,) = kernel_call(
        diagonal_kernel, (), (here,), [(4, quarter, quarter)], 6 * product, found
    )
    sums = [ring_sums(received[i], outs[5 * i + 2 : 5 * i + 4]) for i in range(2)]
    early_parts = [ring_end(outs[5 * i + 4], received[i], sums[i], axes[i]) for i in range(2)]
    early_total = by_slabs(sum_kernel, (), early_parts[0] + early_parts[1], ["both"] * 2, 0)
    outs = chunks(late_kernel, late, (below, below2, above2, diagonal))
    received = [ring_start(*outs[5 * i : 5 * i + 2], axes[i]) for i in range(2)]
    sums = [ring_sums(received[i], outs[5 * i + 2 : 5 * i + 4]) for i in range(2)]
    late_parts = [ring_end(outs[5 * i + 4], received[i], sums[i], axes[i]) for i in range(2)]
    outs = by_slabs(
        finish_kernel,
        (device, jnp.asarray(ahead.reshape(-1))),
        (early_total[0], *late_parts[0], early_total[1], *late_parts[1]),
        ["one"] * 8,
        1,
    )
    parts = direct(outs[:4], shift_y) + direct(outs[4:], shift_x)
    one, two = kernel_call(
        mirror_kernel,
        (device, jnp.asarray(flags.reshape(-1))),
        parts,
        [(2, quarter, quarter)] * 2,
    )
    one = lax.ppermute(one, ("row", "col"), first)
    two = lax.ppermute(two, ("row", "col"), second)
    one_is_right = jnp.asarray(half)[device_index] == 1
    left = jnp.where(one_is_right, two, one)
    right = jnp.where(one_is_right, one, two)
    real = jnp.concatenate([left[0], right[0]], axis=1)
    imag = jnp.concatenate([left[1], right[1]], axis=1)
    return real, imag, gain


def starting_gains(initial_gains):
    blocks = SIDE * SIDE // PLANES
    pairs = [
        (r * PLANES + c, (r % blocks * PLANES + c) * PLANES + r // blocks)
        for r in range(SIDE * SIDE)
        for c in range(PLANES)
    ]
    share = lax.ppermute(initial_gains, ("row", "col"), pairs)
    return exchange(share, "row").transpose(1, 0, 2).reshape(2, -1)


def body(samples, sky_model, initial_gains):
    column_count = lax.axis_size("col")
    row_index = lax.axis_index("row")
    column_index = lax.axis_index("col")
    block_column = samples.shape[0]
    block_row = sky_model.shape[0]
    share_size = initial_gains.shape[1]
    blocks = block_column // block_row
    gain = starting_gains(initial_gains)
    vis_real, vis_imag, gain = vis_tiles(samples, gain)
    model_real = sky_model[:, 0, :].astype(jnp.float32)
    model_imag = sky_model[:, 1, :].astype(jnp.float32)
    global_rows = row_index * block_row + lax.broadcasted_iota(
        jnp.int32, (block_row, block_column), 0
    )
    global_columns = column_index * block_column + lax.broadcasted_iota(
        jnp.int32, (block_row, block_column), 1
    )
    cross_mask = (global_rows != global_columns).astype(jnp.float32)
    weight_real = (vis_real * model_real + vis_imag * model_imag) * cross_mask
    weight_imag = (vis_real * model_imag - vis_imag * model_real) * cross_mask
    power = (model_real * model_real + model_imag * model_imag) * cross_mask

    parts = columns_to_rows(weight_real, weight_imag, power, gain)
    sums = jnp.sum(exchange(parts.reshape(-1, 128), "col"), axis=0).reshape(parts.shape)
    gain = sums[:2] / sums[2:]

    parts = rows_to_columns(weight_real, weight_imag, power, gain)
    lanes = 128
    message = jnp.concatenate([parts.reshape(-1, lanes), gain.reshape(-1, lanes)])
    received = exchange(message, "row")
    count = parts.size // lanes
    sums = jnp.sum(received, axis=0)[:count].reshape(3, block_column)
    previous = lax.dynamic_slice(
        received, (column_index * blocks, count, 0), (blocks, gain.size // lanes, lanes)
    )
    previous = previous.reshape(blocks, 2, -1, lanes).transpose(1, 0, 2, 3).reshape(2, block_column)
    gain = 0.5 * (sums[:2] / sums[2:] + previous)

    parts = columns_to_rows(weight_real, weight_imag, power, gain)
    shares = parts.reshape(3, column_count, share_size).transpose(1, 0, 2)
    sums = jnp.sum(lax.all_to_all(shares, "col", 0, 0), axis=0)
    return sums[:2] / sums[2:]


def solution(mesh):
    return jax.shard_map(
        body,
        mesh=mesh,
        in_specs=(
            P(("chan", "col"), None, "row"),
            P(("chan", "row"), None, "col"),
            P(None, ("chan", "row", "col")),
        ),
        out_specs=P(None, ("chan", "row", "col")),
        check_vma=False,
    )
```

```python
import jax
import jax.numpy as jnp
import numpy as np
from jax import lax
from jax.experimental import pallas as pl
from jax.experimental.pallas import tpu as pltpu
from jax.sharding import PartitionSpec as P


SIDE = 4
PLANES = 8

OFFSETS = {0: (0, 0), 1: (0, 1), 2: (-1, 1), 3: (-1, 2), 4: (-2, 2)}
EARLY = [(d, h, k) for d in (1, 2) for h in (0, 1) for k in (0, 1)]
LATE = [(3, h, k) for h in (0, 1) for k in (0, 1)] + [(4, 0, 0), (4, 1, 1), (0, 0, 0), (0, 0, 1)]
PLACE = [
    [7, 0, 2, 5, 13, 10, 8, 15, 14, 6, 3, 12, 11, 9, 1, 4],
    [15, 10, 8, 2, 0, 7, 5, 13, 9, 4, 1, 14, 6, 11, 12, 3],
    [13, 8, 5, 10, 2, 0, 7, 15, 11, 14, 3, 1, 12, 9, 6, 4],
    [10, 13, 15, 2, 0, 8, 7, 5, 11, 4, 14, 9, 1, 12, 3, 6],
    [15, 8, 13, 10, 2, 5, 7, 0, 11, 6, 4, 14, 3, 1, 12, 9],
    [2, 10, 15, 0, 8, 5, 7, 13, 11, 12, 14, 9, 3, 1, 6, 4],
    [15, 0, 2, 13, 5, 8, 10, 7, 9, 14, 3, 11, 6, 4, 1, 12],
    [2, 5, 7, 10, 8, 0, 15, 13, 3, 12, 9, 1, 4, 6, 11, 14],
]


def targets(chunk, c):
    d, h, k = chunk
    a, b = [(c + offset) % PLANES for offset in OFFSETS[d]]
    if d == 0 and k == 0:
        return (2 * c, c, 0), (2 * c + 1, c, 1), 0
    if d == 0:
        return (2 * c + 1, c, 0), (2 * c, c, 1), 1
    if d == 4:
        k = h if c < PLANES // 2 else 1 - h
    plain, mirror = (2 * a + h, b, k), (2 * b + k, a, h)
    if d == 4 or h == k:
        return plain, mirror, 0
    return mirror, plain, 1


def tables():
    rows = SIDE * SIDE
    devices = rows * PLANES
    first, second = [], []
    early = np.zeros((devices, 2, SIDE, 2), np.int32)
    late = np.zeros((devices, 2, SIDE, 2), np.int32)
    ahead = np.zeros((devices, 2, SIDE), np.int32)
    flags = np.zeros((devices, 2), np.int32)
    half = np.zeros(devices, np.int32)
    for c in range(PLANES):
        for chunk, r in zip(EARLY + LATE, PLACE[c]):
            one, two, conjugated = targets(chunk, c)
            first.append((r * PLANES + c, one[0] * PLANES + one[1]))
            second.append((r * PLANES + c, two[0] * PLANES + two[1]))
            flags[r * PLANES + c] = conjugated, chunk == (0, 0, 0)
            half[one[0] * PLANES + one[1]] = one[2]
        for i, owner in enumerate(PLACE[c]):
            v, u = owner // SIDE, owner % SIDE
            order, index = (early, i) if i < len(EARLY) else (late, i - len(EARLY))
            for r in range(rows):
                y, x = r // SIDE, r % SIDE
                order[r * PLANES + c, 0, (u - x) % SIDE, v // 2] = index
                order[r * PLANES + c, 1, (v - y) % SIDE, u // 2] = index
        for r in range(rows):
            y, x = r // SIDE, r % SIDE
            for t in range(SIDE):
                v, u = (y + t) % SIDE, (x + t) % SIDE
                ahead[r * PLANES + c, 0, t] = (v + x) % 2 * 2 + v // 2
                ahead[r * PLANES + c, 1, t] = (u + y) % 2 * 2 + u // 2
    return first, second, early, late, ahead, flags, half


def matmul(lhs, rhs):
    return lax.dot_general(lhs, rhs, (((1,), (1,)), ((), ())), preferred_element_type=jnp.float32)


def rows_of(ref, half):
    quarter = ref.shape[0] // 2
    return ref[pl.ds(pl.multiple_of(half * quarter, quarter), quarter), :]


def slabs(rows, count=4):
    def run(function):
        @pl.loop(0, count)
        def _(i):
            function(pl.ds(pl.multiple_of(i * (rows // count), rows // count), rows // count))

    return run


def turn(out, block):
    times = block.shape[1] // 2

    @slabs(block.shape[0])
    def _(rows):
        out[rows, :times] = -block[rows, times:]
        out[rows, times:] = block[rows, :times]


def diagonal_kernel(block, out, turned, found):
    turn(turned, block)
    for part, rhs in enumerate((block, turned)):

        @pl.loop(0, 3)
        def _(i):
            lhs = rows_of(block, jnp.where(i == 1, 1, 0))
            found[2 * i + part] = matmul(lhs, rows_of(rhs, jnp.where(i == 0, 0, 1)))

    out[0] = found[0] + found[1]
    out[1] = found[2] + found[3]
    out[2], out[3] = found[4], found[5]


ORDER = ((2, 0), (1, 1), (2, 1), (3, 0), (1, 0), (3, 1), (0, 0), (0, 1))


def stores(right, left, up, down, own):
    return {
        (0, 0): own.at[0],
        (0, 1): own.at[1],
        (1, 0): up,
        (1, 1): right.at[1],
        (2, 0): right.at[0],
        (2, 1): left.at[0],
        (3, 0): left.at[1],
        (3, 1): down,
    }


def stack(lefts, one, two):
    @slabs(one.shape[0])
    def _(rows):
        lefts[0, rows], lefts[1, rows] = one[rows], two[rows]


def early_kernel(device, table, one, two, block, *refs):
    outs, lefts, turned = refs[:10], refs[10], refs[11]
    stack(lefts, one, two)
    turn(turned, block)
    for t, j in ORDER:
        for color, rhs in enumerate((block, turned)):
            index = table[device[0] * 16 + color * 8 + t * 2 + j]
            lhs = rows_of(lefts.at[index // 4], index // 2 % 2)
            out = stores(*outs[5 * color : 5 * color + 5])[t, j]
            out[...] = matmul(lhs, rows_of(rhs, index % 2))


def late_kernel(device, table, one, two, block, diagonal, *refs):
    outs, lefts, turned = refs[:10], refs[10], refs[11]
    stack(lefts, one, two)
    turn(turned, block)
    upper = (device[1] >= PLANES // 2).astype(jnp.int32)
    for t, j in ORDER:
        for color, rhs in enumerate((block, turned)):
            index = table[device[0] * 16 + color * 8 + t * 2 + j]
            near = index < 4
            h = jnp.where(near, index // 2, index % 2)
            k = jnp.where(near, index % 2, (h + upper) % 2)
            product = matmul(rows_of(lefts.at[index // 4], h), rows_of(rhs, k))
            ready = diagonal[jnp.maximum(index - 6, 0) * 2 + color]
            out = stores(*outs[5 * color : 5 * color + 5])[t, j]
            out[...] = jnp.where(index < 6, product, ready)


def sum_kernel(*refs):
    for color in range(2):
        own, right, left, right2, left2 = refs[5 * color : 5 * color + 5]
        refs[10 + color][0] = own[0] + right2[...] + left[0]
        refs[10 + color][1] = own[1] + right[0] + left2[...]


def finish_kernel(device, ahead, *refs):
    ins, outs, sums = refs[:12], refs[12:20], refs[20]
    for color in range(2):
        early, own, right, left, right2, left2 = ins[6 * color : 6 * color + 6]
        sums[0], sums[1] = early[0], early[1]
        sums[2] = own[0] + right2[...] + left[0]
        sums[3] = own[1] + right[0] + left2[...]
        for t in range(SIDE):
            outs[4 * color + t][...] = sums[ahead[device[0] * 8 + color * 4 + t]]


def by_slabs(kernel, scalars, parts, outs, scratch, steps=4):
    quarter = parts[0].shape[-1]
    slab = quarter // steps
    specs = {
        "one": pl.BlockSpec((slab, quarter), lambda i: (i, 0)),
        "second": pl.BlockSpec((1, slab, quarter), lambda i: (1, i, 0)),
        "both": pl.BlockSpec((2, slab, quarter), lambda i: (0, i, 0)),
    }
    pattern = ["both", "second", "second", "one", "one"]
    if len(parts) == 12:
        pattern = ["both"] + pattern
    size = {"one": (quarter, quarter), "both": (2, quarter, quarter)}
    return pl.pallas_call(
        kernel,
        grid=(steps,),
        out_shape=[jax.ShapeDtypeStruct(size[out], jnp.float32) for out in outs],
        in_specs=[pl.BlockSpec(memory_space=pltpu.SMEM)] * len(scalars) + [specs[p] for p in 2 * pattern],
        out_specs=[specs[out] for out in outs],
        scratch_shapes=[pltpu.VMEM((4, slab, quarter), jnp.float32)] * scratch,
        cost_estimate=pl.CostEstimate(
            flops=8 * quarter * quarter, bytes_accessed=72 * quarter * quarter, transcendentals=0
        ),
    )(*scalars, *parts)


def mirror_kernel(device, flags, *refs):
    p, q = [(refs[i][...] + refs[i + 2][...]) + (refs[i + 1][...] + refs[i + 3][...]) for i in (0, 4)]
    first, second = refs[8:]
    pt, qt = p.T, q.T
    flip = flags[device[0] * 2] == 1
    diagonal = flags[device[0] * 2 + 1] == 1
    first[0] = jnp.where(diagonal, 0.5 * (p + pt), jnp.where(flip, pt, p))
    first[1] = jnp.where(diagonal, 0.5 * (p - pt), jnp.where(flip, -qt, q))
    second[0] = jnp.where(diagonal, 0.5 * (q + qt), jnp.where(flip, p, pt))
    second[1] = jnp.where(diagonal, 0.5 * (q - qt), jnp.where(flip, q, -qt))


def kernel_call(kernel, scalars, blocks, shapes, flops=0, scratch=()):
    shapes = [jax.ShapeDtypeStruct(shape, jnp.float32) for shape in shapes]
    vmem = pl.BlockSpec(memory_space=pltpu.VMEM)
    smem = pl.BlockSpec(memory_space=pltpu.SMEM)
    moved = sum(v.size * v.dtype.itemsize for v in blocks) + sum(4 * v.size for v in shapes)
    return pl.pallas_call(
        kernel,
        out_shape=shapes,
        in_specs=[smem] * len(scalars) + [vmem] * len(blocks),
        out_specs=[vmem] * len(shapes),
        scratch_shapes=scratch,
        cost_estimate=pl.CostEstimate(flops=flops, bytes_accessed=moved, transcendentals=0),
    )(*scalars, *blocks)


def shift_x(value, step):
    pairs = [
        (y * SIDE + x, y * SIDE + (x + step) % SIDE) for y in range(SIDE) for x in range(SIDE)
    ]
    return lax.ppermute(value, "row", pairs)


def shift_y(value, step):
    pairs = [
        (y * SIDE + x, (y + step) % SIDE * SIDE + x) for y in range(SIDE) for x in range(SIDE)
    ]
    return lax.ppermute(value, "row", pairs)


def shift_z(value, step):
    return lax.ppermute(value, "col", [(c, (c + step) % PLANES) for c in range(PLANES)])


def ring_start(right, left, shift):
    return shift(right, 1), shift(left, -1)


def ring_sums(received, rest):
    right, left = received
    return rest[0] + right[0], rest[1] + left[0]


def ring_end(own, received, sums, shift):
    return own, *received, shift(sums[0], 1), shift(sums[1], -1)


def direct(outs, shift):
    return (outs[0],) + tuple(shift(outs[t], t) for t in range(1, SIDE))


def exchange(parts, axis):
    count = lax.axis_size(axis)
    copies = jnp.broadcast_to(parts[None], (count,) + parts.shape)
    return lax.all_to_all(copies, axis, 0, 0)


def columns_to_rows(weight_real, weight_imag, power, gain):
    real = gain[0][None, :]
    imag = gain[1][None, :]
    return jnp.stack(
        [
            jnp.sum(weight_real * real + weight_imag * imag, axis=1),
            jnp.sum(weight_real * imag - weight_imag * real, axis=1),
            jnp.sum(power * (real * real + imag * imag), axis=1),
        ]
    )


def rows_to_columns(weight_real, weight_imag, power, gain):
    real = gain[0][:, None]
    imag = gain[1][:, None]
    return jnp.stack(
        [
            jnp.sum(weight_real * real - weight_imag * imag, axis=0),
            jnp.sum(weight_real * imag + weight_imag * real, axis=0),
            jnp.sum(power * (real * real + imag * imag), axis=0),
        ]
    )


def vis_tiles(here, gain):
    row_index = lax.axis_index("row")
    column_index = lax.axis_index("col")
    first, second, early, late, ahead, flags, half = tables()
    device_index = row_index * PLANES + column_index
    device = jnp.stack([device_index, column_index]).astype(jnp.int32)
    antennas, times = here.shape
    quarter = antennas // 2
    product = 2 * quarter * quarter * times
    turned = pltpu.VMEM(here.shape, here.dtype)
    stacks = pltpu.VMEM((2,) + here.shape, here.dtype), turned
    found = turned, pltpu.VMEM((6, quarter, quarter), jnp.float32)
    above, below = shift_z(here, -1), shift_z(here, 1)
    gain, above, below = lax.optimization_barrier((gain, above, below))
    above2, below2 = shift_z(above, -1), shift_z(below, 1)
    shapes = 2 * ([(2, quarter, quarter)] * 2 + [(quarter, quarter)] * 2 + [(2, quarter, quarter)])
    axes = (shift_x, shift_y)

    def chunks(kernel, table, blocks):
        scalars = device, jnp.asarray(table.reshape(-1))
        return kernel_call(kernel, scalars, blocks, shapes, 16 * product, stacks)

    outs = chunks(early_kernel, early, (here, below, above))
    received = [ring_start(*outs[5 * i : 5 * i + 2], axes[i]) for i in range(2)]
    (diagonal,) = kernel_call(
        diagonal_kernel, (), (here,), [(4, quarter, quarter)], 6 * product, found
    )
    sums = [ring_sums(received[i], outs[5 * i + 2 : 5 * i + 4]) for i in range(2)]
    early_parts = [ring_end(outs[5 * i + 4], received[i], sums[i], axes[i]) for i in range(2)]
    early_total = by_slabs(sum_kernel, (), early_parts[0] + early_parts[1], ["both"] * 2, 0)
    outs = chunks(late_kernel, late, (below, below2, above2, diagonal))
    received = [ring_start(*outs[5 * i : 5 * i + 2], axes[i]) for i in range(2)]
    sums = [ring_sums(received[i], outs[5 * i + 2 : 5 * i + 4]) for i in range(2)]
    late_parts = [ring_end(outs[5 * i + 4], received[i], sums[i], axes[i]) for i in range(2)]
    outs = by_slabs(
        finish_kernel,
        (device, jnp.asarray(ahead.reshape(-1))),
        (early_total[0], *late_parts[0], early_total[1], *late_parts[1]),
        ["one"] * 8,
        1,
    )
    parts = direct(outs[:4], shift_y) + direct(outs[4:], shift_x)
    one, two = kernel_call(
        mirror_kernel,
        (device, jnp.asarray(flags.reshape(-1))),
        parts,
        [(2, quarter, quarter)] * 2,
    )
    one = lax.ppermute(one, ("row", "col"), first)
    two = lax.ppermute(two, ("row", "col"), second)
    one_is_right = jnp.asarray(half)[device_index] == 1
    left = jnp.where(one_is_right, two, one)
    right = jnp.where(one_is_right, one, two)
    real = jnp.concatenate([left[0], right[0]], axis=1)
    imag = jnp.concatenate([left[1], right[1]], axis=1)
    return real, imag, gain


def starting_gains(initial_gains):
    blocks = SIDE * SIDE // PLANES
    pairs = [
        (r * PLANES + c, (r % blocks * PLANES + c) * PLANES + r // blocks)
        for r in range(SIDE * SIDE)
        for c in range(PLANES)
    ]
    share = lax.ppermute(initial_gains, ("row", "col"), pairs)
    return exchange(share, "row").transpose(1, 0, 2).reshape(2, -1)


def body(samples, sky_model, initial_gains):
    column_count = lax.axis_size("col")
    row_index = lax.axis_index("row")
    column_index = lax.axis_index("col")
    block_column = samples.shape[0]
    block_row = sky_model.shape[0]
    share_size = initial_gains.shape[1]
    blocks = block_column // block_row
    flattened = samples.reshape(block_column, -1)
    flattened, first_gains = lax.optimization_barrier((flattened, initial_gains))
    gain = starting_gains(first_gains)
    vis_real, vis_imag, gain = vis_tiles(flattened, gain)
    model_real = sky_model[:, 0, :].astype(jnp.float32)
    model_imag = sky_model[:, 1, :].astype(jnp.float32)
    global_rows = row_index * block_row + lax.broadcasted_iota(
        jnp.int32, (block_row, block_column), 0
    )
    global_columns = column_index * block_column + lax.broadcasted_iota(
        jnp.int32, (block_row, block_column), 1
    )
    cross_mask = (global_rows != global_columns).astype(jnp.float32)
    weight_real = (vis_real * model_real + vis_imag * model_imag) * cross_mask
    weight_imag = (vis_real * model_imag - vis_imag * model_real) * cross_mask
    power = (model_real * model_real + model_imag * model_imag) * cross_mask

    parts = columns_to_rows(weight_real, weight_imag, power, gain)
    sums = jnp.sum(exchange(parts.reshape(-1, 128), "col"), axis=0).reshape(parts.shape)
    gain = sums[:2] / sums[2:]

    parts = rows_to_columns(weight_real, weight_imag, power, gain)
    lanes = 128
    message = jnp.concatenate([parts.reshape(-1, lanes), gain.reshape(-1, lanes)])
    received = exchange(message, "row")
    count = parts.size // lanes
    sums = jnp.sum(received, axis=0)[:count].reshape(3, block_column)
    previous = lax.dynamic_slice(
        received, (column_index * blocks, count, 0), (blocks, gain.size // lanes, lanes)
    )
    previous = previous.reshape(blocks, 2, -1, lanes).transpose(1, 0, 2, 3).reshape(2, block_column)
    gain = 0.5 * (sums[:2] / sums[2:] + previous)

    parts = columns_to_rows(weight_real, weight_imag, power, gain)
    shares = parts.reshape(3, column_count, share_size).transpose(1, 0, 2)
    sums = jnp.sum(lax.all_to_all(shares, "col", 0, 0), axis=0)
    return sums[:2] / sums[2:]


def solution(mesh):
    return jax.shard_map(
        body,
        mesh=mesh,
        in_specs=(
            P(("chan", "col"), None, "row"),
            P(("chan", "row"), None, "col"),
            P(None, ("chan", "row", "col")),
        ),
        out_specs=P(None, ("chan", "row", "col")),
        check_vma=False,
    )
```
